256 devices in a mesh: tm: 16 (over x, y), pairs: 16 (over z, core).
Axes of the slice: x: 4, y: 4, z: 8, core: 2. Of those that a mesh axis runs over, the one named last changes fastest.
Arguments:
- panels: bfloat16 [48, 16, 1024, 128], P('tm', None, 'pairs')
- pair_list: int32 [2, 262144], P(None, ('tm', 'pairs')), may hold values from 0 to 16383, as said below
- pair_count: int32 [256], P(('tm', 'pairs')), may hold values from 1 to 1024, as said below
Outputs:
- stacks: float32 [262144, 512], P(('tm', 'pairs'))
The draws below stay inside these ranges and needn't reach their ends.
Inputs may be any that keep to these rules, and one draw needn't show every extreme that they name: `pair_list`: slots o * 1024 to (o + 1) * 1024 - 1 belong to owner o. The first channel of each is one of channels o * 64 to (o + 1) * 64 - 1; the second lies 1 to 100 channels after it, in the same section of 1024 channels. A distance of 100 occurs in every draw. Owner o's live slots are its first pair_count[o]. Some owner has all 1024 live in every draw.
All inputs are finite; a program needn't handle non-finite values.
Results may differ from the reference program's by a relative error of at most 0.015.
Values may be sent and summed in bfloat16 or wider, within the bound.
No kernel may reach another device: no remote copies, remote signals or barrier semaphores. Data moves between devices by JAX's collectives and lax.ppermute only.
A program may use at most 128 MiB of HBM per device.

```python
import math
import jax
import jax.numpy as jnp
from jax import lax

CH_DEV = 64
NB = 100
SEG = 512
SEGS = 12
TILE = 128
PAIR_CAP = 1024
SECTIONS = 16
SECTION = 1024
OWNERS = 256
CHANNELS = 16384
NTILE = 48


def draw_panels(key, part):
    subkeys = jax.random.split(key, 3)
    full_shape = (NTILE, SECTIONS, SECTION, TILE)
    noise_part = jax.random.normal(subkeys[0], full_shape, jnp.float32)
    channel_scale = jnp.exp(jax.random.uniform(subkeys[1], (1, SECTIONS, SECTION, 1), jnp.float32, 0.0, jnp.log(10.0)))
    tile_scale = jnp.exp(jax.random.uniform(subkeys[2], (NTILE, SECTIONS, SECTION, 1), jnp.float32, 0.0, jnp.log(10.0)))
    return (noise_part * channel_scale * tile_scale).astype(jnp.bfloat16)


def draw_pair_list(key, part):
    subkeys = jax.random.split(key, 2)
    slot_ids = jnp.arange(OWNERS * PAIR_CAP, dtype=jnp.int32)
    owner_ids = slot_ids // PAIR_CAP
    within = owner_ids % (SECTION // CH_DEV)
    last_block = (within == SECTION // CH_DEV - 1).astype(jnp.int32)
    local_first = jax.random.randint(subkeys[0], slot_ids.shape, 0, CH_DEV - last_block)
    position = within * CH_DEV + local_first
    reach_max = jnp.minimum(SECTION - 1 - position, NB)
    raw_step = jax.random.randint(subkeys[1], slot_ids.shape, 0, 1 << 20)
    distance = 1 + raw_step % reach_max
    distance = jnp.where(slot_ids % PAIR_CAP == 0, reach_max, distance)
    firsts = owner_ids * CH_DEV + local_first
    return jnp.stack([firsts, firsts + distance]).astype(jnp.int32)


def draw_pair_count(key, part):
    subkeys = jax.random.split(key, 3)
    base_count = jax.random.randint(subkeys[0], (OWNERS,), PAIR_CAP // 4, PAIR_CAP + 1)
    divisor = 1 + jax.random.randint(subkeys[1], (OWNERS,), 0, 3)
    counts = base_count // divisor
    busiest = jax.random.randint(subkeys[2], (), 0, OWNERS)
    counts = jnp.where(jnp.arange(OWNERS, dtype=jnp.int32) == busiest, PAIR_CAP, counts)
    return counts.astype(jnp.int32)


def setup_inputs(seed: int = 0) -> dict:
    key_of = jax.random.split(jax.random.key(seed), 4)
    panels = draw_panels(jax.random.fold_in(key_of[3], 71), 0)
    pair_list = draw_pair_list(jax.random.fold_in(key_of[3], 71), 0)
    pair_count = draw_pair_count(jax.random.fold_in(key_of[3], 71), 0)
    return {"panels": panels, "pair_list": pair_list, "pair_count": pair_count}


def reference(panels, pair_list, pair_count):
    samples = jnp.transpose(panels, (1, 2, 0, 3)).reshape(CHANNELS, SEGS, SEG).astype(jnp.float32)
    mean_square = lax.optimization_barrier(jnp.mean(samples * samples, axis=2, keepdims=True))
    scaled = lax.optimization_barrier((samples * lax.rsqrt(mean_square + 1e-05)).astype(jnp.bfloat16))
    spectrum = jnp.fft.rfft(scaled.astype(jnp.float32), n=2 * SEG, axis=2)[:, :, :SEG] / math.sqrt(SEG)
    real_part = jnp.real(spectrum)
    imag_part = jnp.imag(spectrum)
    level_power = lax.optimization_barrier(jnp.mean(real_part * real_part + imag_part * imag_part, axis=1, keepdims=True))
    weight_gain = 1.0 / jnp.sqrt(level_power + 0.5)
    whitened = jnp.concatenate([real_part * weight_gain, imag_part * weight_gain], axis=2).astype(jnp.bfloat16)
    firsts = pair_list[0].reshape(OWNERS, PAIR_CAP)
    seconds = pair_list[1].reshape(OWNERS, PAIR_CAP)

    def one_owner(pair_block):
        first_ids, second_ids, live_count = pair_block
        left_rows = jnp.take(whitened, first_ids, axis=0).astype(jnp.float32)
        right_rows = jnp.take(whitened, second_ids, axis=0).astype(jnp.float32)
        left_real = left_rows[:, :, :SEG]
        left_imag = left_rows[:, :, SEG:]
        right_real = right_rows[:, :, :SEG]
        right_imag = right_rows[:, :, SEG:]
        cross_real = lax.optimization_barrier(jnp.mean(left_real * right_real + left_imag * right_imag, axis=1))
        cross_imag = lax.optimization_barrier(jnp.mean(left_imag * right_real - left_real * right_imag, axis=1))
        cross_spec = lax.optimization_barrier(jnp.concatenate([cross_real, cross_imag], axis=1).astype(jnp.bfloat16))
        cross_spec = cross_spec.astype(jnp.float32)
        spectrum_full = cross_spec[:, :SEG] + 1j * cross_spec[:, SEG:]
        spectrum_full = jnp.pad(spectrum_full, ((0, 0), (0, 1)))
        lagged = jnp.fft.irfft(spectrum_full, n=2 * SEG, axis=1) * (2 * SEG) / math.sqrt(SEG)
        lagged = jnp.concatenate([lagged[:, 2 * SEG - SEG // 2:], lagged[:, :SEG // 2]], axis=1)
        live_mask = jnp.arange(PAIR_CAP, dtype=jnp.int32) < live_count
        return jnp.where(live_mask[:, None], lagged, 0.0).astype(jnp.float32)
    result = lax.map(one_owner, (firsts, seconds, pair_count))
    return result.reshape(OWNERS * PAIR_CAP, SEG)
```

```python
import math
import numpy as np
import ml_dtypes
import jax, jax.numpy as jnp
from jax import lax
from jax.sharding import PartitionSpec as P
from jax.experimental import pallas as pl
from jax.experimental.pallas import tpu as pltpu

SEG=512; SEGS=12; CAP=1024
def tables():
    u=np.arange(SEG)[:,None]; k=np.arange(SEG)[None,:]
    a=(u*k%(2*SEG))*(math.pi/SEG)
    fwd=np.concatenate([np.cos(a),-np.sin(a)],axis=1)/math.sqrt(SEG)
    k=np.arange(SEG)[:,None]; m=np.arange(SEG)[None,:]-SEG//2
    a=(k*m%(2*SEG))*(math.pi/SEG)
    w=np.where(k==0,1.0,2.0)/math.sqrt(SEG)/SEGS
    inv=np.concatenate([w*np.cos(a),-w*np.sin(a)],axis=0)
    return fwd.astype(np.float32).astype(ml_dtypes.bfloat16), inv.astype(np.float32).astype(ml_dtypes.bfloat16)

NCH=168
MB=336
U=8
ROWS=SEGS*8
def kernel(idx_ref, cnt_ref, own_ref, h1_ref, h2_ref, fwd_ref, inv_ref, out_ref, scaled, spec, cr, ci):
    for s in range(SEGS):
        base=0
        for ref in (own_ref,h1_ref,h2_ref):
            C=ref.shape[1]
            x=[ref[4*s+q].astype(jnp.float32) for q in range(4)]
            ss=x[0]*x[0]+x[1]*x[1]+x[2]*x[2]+x[3]*x[3]
            g=lax.rsqrt(jnp.sum(ss,axis=1,keepdims=True)*(1.0/SEG)+1e-5)
            for q in range(4):
                scaled[pl.ds(s*NCH+base,C),q*128:(q+1)*128]=(x[q]*g).astype(jnp.bfloat16)
            base+=C
    for b in range(SEGS*NCH//MB):
        spectrum=jnp.dot(scaled[pl.ds(b*MB,MB),:],fwd_ref[...],preferred_element_type=jnp.float32)
        for t in range(MB//NCH):
            s=b*(MB//NCH)+t
            for c in range(8):
                part,g=divmod(c,4)
                row=(part*6+s//2)*8+(s%2)*4+g
                spec[pl.ds(row,NCH,stride=ROWS),:]=spectrum[t*NCH:(t+1)*NCH,c*128:(c+1)*128]
    def whiten(ch,_):
        v=[spec[pl.ds(ch*ROWS+r*8,8),:] for r in range(12)]
        lev=v[0]*v[0]
        for r in range(1,12): lev=lev+v[r]*v[r]
        lev=lev+pltpu.roll(lev,4,0)
        g=lax.rsqrt(lev*(1.0/SEGS)+0.5)
        for r in range(12):
            spec[pl.ds(ch*ROWS+r*8,8),:]=v[r]*g
        return 0
    lax.fori_loop(0,NCH,whiten,0,unroll=4)
    def pairs(n,_):
        for t in range(U):
            p=n*U+t
            i=pl.multiple_of(idx_ref[0,p],8); j=pl.multiple_of(idx_ref[1,p],8)
            are=None
            for h in range(6):
                lr=spec[pl.ds(i+h*8,8),:]; li=spec[pl.ds(i+(6+h)*8,8),:]
                rr=spec[pl.ds(j+h*8,8),:]; ri=spec[pl.ds(j+(6+h)*8,8),:]
                if are is None:
                    are=lr*rr+li*ri; aim=li*rr-lr*ri
                else:
                    are=are+lr*rr+li*ri; aim=aim+li*rr-lr*ri
            cr[pl.ds(p*8,8),:]=are
            ci[pl.ds(p*8,8),:]=aim
        return 0
    lax.fori_loop(0,CAP//U,pairs,0)
    PB=256
    for b in range(CAP//PB):
        cols=[]
        for ref in (cr,ci):
            for g in range(4):
                a=ref[pl.ds(b*PB*8+g,PB,stride=8),:]+ref[pl.ds(b*PB*8+g+4,PB,stride=8),:]
                cols.append(a.astype(jnp.bfloat16))
        x=jnp.concatenate(cols,axis=1)
        y=jnp.dot(x,inv_ref[...],preferred_element_type=jnp.float32)
        slot=lax.broadcasted_iota(jnp.int32,(PB,SEG),0)+b*PB
        out_ref[pl.ds(b*PB,PB),:]=jnp.where(slot<cnt_ref[0],y,0.0)

def correlate(idx, cnt, own, h1, h2, fwd, inv):
    V=pl.BlockSpec(memory_space=pltpu.VMEM); S=pl.BlockSpec(memory_space=pltpu.SMEM)
    return pl.pallas_call(kernel,out_shape=jax.ShapeDtypeStruct((CAP,SEG),jnp.float32),
      in_specs=[S,S,V,V,V,V,V],out_specs=V,
      scratch_shapes=[pltpu.VMEM((SEGS*NCH,SEG),jnp.bfloat16),pltpu.VMEM((NCH*ROWS,128),jnp.float32),
         pltpu.VMEM((CAP*8,128),jnp.float32),pltpu.VMEM((CAP*8,128),jnp.float32)],
      compiler_params=pltpu.CompilerParams(vmem_limit_bytes=48<<20))(idx,cnt,own,h1,h2,fwd,inv)


def from_ahead(block, axis, distance):
    devices = range(lax.axis_size(axis))
    route = [(i + distance, i) for i in devices if i + distance in devices]
    return lax.ppermute(block, axis, route)


def per_device(panels, pair_list, pair_count):
    relaid = lax.all_to_all(panels, "tm", split_axis=1, concat_axis=0, tiled=True)
    own = relaid[:, 0]
    channels = own.shape[1]
    h1 = from_ahead(own, "pairs", 1)
    h2 = from_ahead(own[:, :NCH - 2 * channels], "pairs", 2)
    fwd, inv = tables()
    offset = (lax.axis_index("tm") * lax.axis_size("pairs") + lax.axis_index("pairs")) * channels
    idx = (pair_list - offset) * ROWS
    return correlate(idx, pair_count, own, h1, h2, jnp.asarray(fwd), jnp.asarray(inv))


def solution(mesh):
    return jax.shard_map(
        per_device,
        mesh=mesh,
        in_specs=(P("tm", None, "pairs", None), P(None, ("tm", "pairs")), P(("tm", "pairs"))),
        out_specs=P(("tm", "pairs"), None),
        check_vma=False,
    )
```

```python
import math

import jax
import jax.numpy as jnp
import ml_dtypes
import numpy as np
from jax import lax
from jax.experimental import pallas as pl
from jax.experimental.pallas import tpu as pltpu
from jax.sharding import PartitionSpec as P

NB = 100
SEG = 512
SEGS = 12
TILE = 128
QUADS = SEG // TILE
OWN = 64
HALO = 104
REST = HALO - OWN
ROWS = SEGS * 8
PITCH = ROWS + 1
CAP = 1024
UNROLL = 16
JOBS = CAP + UNROLL
BLOCK = 256
VMEM = pl.BlockSpec(memory_space=pltpu.VMEM)
SMEM = pl.BlockSpec(memory_space=pltpu.SMEM)
HBM = pl.BlockSpec(memory_space=pltpu.HBM)


def tables():
    left = np.arange(SEG)[:, None]
    right = np.arange(SEG)[None, :]
    angles = (left * right % (2 * SEG)) * (math.pi / SEG)
    forward = np.concatenate([np.cos(angles), -np.sin(angles)], axis=1) / math.sqrt(SEG)
    angles = (left * (right - SEG // 2) % (2 * SEG)) * (math.pi / SEG)
    weights = np.where(left == 0, 1.0, 2.0) / (math.sqrt(SEG) * SEGS)
    inverse = np.concatenate([weights * np.cos(angles), -weights * np.sin(angles)], axis=0)
    return forward.astype(ml_dtypes.bfloat16), inverse.astype(ml_dtypes.bfloat16)


def spectra(parts, fwd_ref, scaled, loose, spec):
    total = sum(part.shape[1] for part in parts)
    for s in range(SEGS):
        base = s * total
        for part in parts:
            count = part.shape[1]
            tiles = [part[QUADS * s + q].astype(jnp.float32) for q in range(QUADS)]
            squares = sum(tile * tile for tile in tiles)
            power = jnp.sum(squares, axis=1, keepdims=True) * (1.0 / SEG)
            gain = lax.rsqrt(power + 1e-05)
            for q, tile in enumerate(tiles):
                scaled[pl.ds(base, count), q * TILE:(q + 1) * TILE] = (tile * gain).astype(jnp.bfloat16)
            base += count
    for s in range(0, SEGS, 2):
        rows = scaled[pl.ds(s * total, 2 * total), :]
        both = jnp.dot(rows, fwd_ref[...], preferred_element_type=jnp.float32)
        for t in range(2):
            for c in range(2 * QUADS):
                half, g = divmod(c, QUADS)
                row = (half * (SEGS // 2) + s // 2) * 8 + t * QUADS + g
                loose[pl.ds(row, total, stride=PITCH), :] = both[
                    t * total:(t + 1) * total, c * TILE:(c + 1) * TILE]

    def whiten(ch, carry):
        v = [loose[pl.ds(ch * PITCH + r * 8, 8), :] for r in range(SEGS)]
        level = sum(x * x for x in v)
        level = level + pltpu.roll(level, 4, 0)
        gain = lax.rsqrt(level * (1.0 / SEGS) + 0.5)
        for r in range(SEGS):
            spec[pl.ds(pl.multiple_of(ch * ROWS + r * 8, 8), 8), :] = v[r] * gain
        return carry

    lax.fori_loop(0, total, whiten, 0, unroll=4)


def pair_products(job_ref, left_spec, right_spec, cross):
    low_half = lax.broadcasted_iota(jnp.int32, (8, TILE), 0) < QUADS

    def step(n, carry):
        for t in range(UNROLL):
            slot = n * UNROLL + t
            i = pl.multiple_of(job_ref[slot], 8)
            j = pl.multiple_of(job_ref[JOBS + slot], 8)
            row = pl.multiple_of(job_ref[2 * JOBS + slot], 8)
            real = imag = None
            for h in range(SEGS // 2):
                lr = left_spec[pl.ds(i + h * 8, 8), :]
                li = left_spec[pl.ds(i + (SEGS // 2 + h) * 8, 8), :]
                rr = right_spec[pl.ds(j + h * 8, 8), :]
                ri = right_spec[pl.ds(j + (SEGS // 2 + h) * 8, 8), :]
                if real is None:
                    real = lr * rr + li * ri
                    imag = li * rr - lr * ri
                else:
                    real = real + lr * rr + li * ri
                    imag = imag + li * rr - lr * ri
            real = real + pltpu.roll(real, QUADS, 0)
            imag = imag + pltpu.roll(imag, QUADS, 0)
            cross[pl.ds(row, 8), :] = jnp.where(low_half, real, imag)
        return carry

    lax.fori_loop(0, (job_ref[3 * JOBS] + UNROLL - 1) // UNROLL, step, 0)


def order_kernel(pairs_ref, live_ref, offset_ref, near_ref, far_ref):
    offset = offset_ref[0]
    live = live_ref[0]

    def step(p, carry):
        near, far = carry
        i = (pairs_ref[0, p] - offset) * ROWS
        j = (pairs_ref[1, p] - offset) * ROWS
        inside = (j < OWN * ROWS).astype(jnp.int32)
        active = (p < live).astype(jnp.int32)
        near_ref[near] = i
        near_ref[JOBS + near] = jnp.minimum(j, (OWN - 1) * ROWS)
        near_ref[2 * JOBS + near] = p * 8
        far_ref[far] = i
        far_ref[JOBS + far] = jnp.maximum(j - OWN * ROWS, 0)
        far_ref[2 * JOBS + far] = p * 8
        near = near + active * inside
        return near, far + active - active * inside

    near, far = lax.fori_loop(0, CAP, step, (jnp.int32(0), jnp.int32(0)), unroll=8)
    for ref, count in ((near_ref, near), (far_ref, far)):
        for t in range(UNROLL):
            ref[count + t] = 0
            ref[JOBS + count + t] = 0
            ref[2 * JOBS + count + t] = CAP * 8
        ref[3 * JOBS] = count
        ref[3 * JOBS + 1] = live


def near_kernel(job_ref, own_ref, fwd_ref, spec_out, cross_out, scaled, loose, spec, cross, sems):
    spectra([own_ref], fwd_ref, scaled, loose, spec)
    spec_copy = pltpu.make_async_copy(spec, spec_out, sems.at[0])
    spec_copy.start()
    pair_products(job_ref, spec, spec, cross)
    cross_copy = pltpu.make_async_copy(cross, cross_out, sems.at[1])
    cross_copy.start()
    spec_copy.wait()
    cross_copy.wait()


def far_kernel(job_ref, h1_ref, h2_ref, spec_in, cross_in, fwd_ref, inv_ref, out_ref,
               scaled, loose, halo, spec, cross, stacks, sems):
    spec_copy = pltpu.make_async_copy(spec_in, spec, sems.at[0])
    cross_copy = pltpu.make_async_copy(cross_in, cross, sems.at[1])
    spec_copy.start()
    cross_copy.start()
    spectra([h1_ref, h2_ref], fwd_ref, scaled, loose, halo)
    spec_copy.wait()
    cross_copy.wait()
    pair_products(job_ref, spec, halo, cross)
    live = job_ref[3 * JOBS + 1]
    copies = []
    for b in range(CAP // BLOCK):
        rows = pl.ds(b * BLOCK, BLOCK)

        @pl.when(b * BLOCK < live)
        def _():
            columns = [cross[pl.ds(b * BLOCK * 8 + g, BLOCK, stride=8), :].astype(jnp.bfloat16) for g in range(8)]
            lagged = jnp.dot(
                jnp.concatenate(columns, axis=1), inv_ref[...], preferred_element_type=jnp.float32)
            slot = lax.broadcasted_iota(jnp.int32, (BLOCK, SEG), 0) + b * BLOCK
            stacks[rows, :] = jnp.where(slot < live, lagged, 0.0)

        @pl.when(b * BLOCK >= live)
        def _():
            stacks[rows, :] = jnp.zeros((BLOCK, SEG), jnp.float32)

        copies.append(pltpu.make_async_copy(stacks.at[rows, :], out_ref.at[rows, :], sems.at[2 + b]))
        copies[-1].start()
    for copy in copies:
        copy.wait()


def ints(*shape):
    return jax.ShapeDtypeStruct(shape, jnp.int32)


def floats(*shape):
    return jax.ShapeDtypeStruct(shape, jnp.float32)


CROSS = ((CAP + 1) * 8, TILE)


def order_pairs(pair_list, live, offset):
    return pl.pallas_call(
        order_kernel,
        out_shape=(ints(3 * JOBS + 16), ints(3 * JOBS + 16)),
        in_specs=[SMEM] * 3,
        out_specs=(SMEM,) * 2,
        name="order_pairs",
    )(pair_list, live, offset)


def near_pairs(jobs, own, fwd):
    return pl.pallas_call(
        near_kernel,
        out_shape=(floats(OWN * ROWS, TILE), floats(*CROSS)),
        in_specs=[SMEM, VMEM, VMEM],
        out_specs=(HBM,) * 2,
        scratch_shapes=[
            pltpu.VMEM((SEGS * OWN, SEG), jnp.bfloat16),
            pltpu.VMEM((OWN * PITCH + 8, TILE), jnp.float32),
            pltpu.VMEM((OWN * ROWS, TILE), jnp.float32),
            pltpu.VMEM(CROSS, jnp.float32),
            pltpu.SemaphoreType.DMA((2,)),
        ],
        compiler_params=pltpu.CompilerParams(vmem_limit_bytes=60 << 20),
        name="near_pairs",
    )(jobs, own, fwd)


def far_pairs(jobs, h1, h2, spec, cross, fwd, inv):
    return pl.pallas_call(
        far_kernel,
        out_shape=floats(CAP, SEG),
        in_specs=[SMEM, VMEM, VMEM, HBM, HBM, VMEM, VMEM],
        out_specs=HBM,
        scratch_shapes=[
            pltpu.VMEM((SEGS * HALO, SEG), jnp.bfloat16),
            pltpu.VMEM((HALO * PITCH + 8, TILE), jnp.float32),
            pltpu.VMEM((HALO * ROWS, TILE), jnp.float32),
            pltpu.VMEM((OWN * ROWS, TILE), jnp.float32),
            pltpu.VMEM(CROSS, jnp.float32),
            pltpu.VMEM((CAP, SEG), jnp.float32),
            pltpu.SemaphoreType.DMA((2 + CAP // BLOCK,)),
        ],
        compiler_params=pltpu.CompilerParams(vmem_limit_bytes=60 << 20),
        name="far_pairs",
    )(jobs, h1, h2, spec, cross, fwd, inv)


def from_ahead(block, axis, distance):
    devices = range(lax.axis_size(axis))
    route = [(i + distance, i) for i in devices if i + distance in devices]
    return lax.ppermute(block, axis, route)


def by_section(block):
    rows = lax.all_to_all(block, "tm", split_axis=0, concat_axis=0, tiled=True)
    return rows.reshape(-1, *block.shape[2:])


def per_device(panels, pair_list, pair_count):
    fwd, inv = (jnp.asarray(table) for table in tables())
    offset = (lax.axis_index("tm") * lax.axis_size("pairs") + lax.axis_index("pairs")) * OWN
    near, far = order_pairs(pair_list, pair_count, offset.astype(jnp.int32)[None])
    turned = jnp.transpose(panels, (1, 0, 2, 3))
    h2_turned = from_ahead(turned[:, :, :REST], "pairs", 2)
    own = by_section(turned)
    own, near, far = lax.optimization_barrier((own, near, far))
    h1 = from_ahead(own, "pairs", 1)
    h2 = by_section(h2_turned)
    spec, cross = near_pairs(near, own, fwd)
    return far_pairs(far, h1, h2, spec, cross, fwd, inv)


def solution(mesh):
    return jax.shard_map(
        per_device,
        mesh=mesh,
        in_specs=(P("tm", None, "pairs", None), P(None, ("tm", "pairs")), P(("tm", "pairs"))),
        out_specs=P(("tm", "pairs"), None),
        check_vma=False,
    )
```

```python
import math

import jax
import jax.numpy as jnp
import ml_dtypes
import numpy as np
from jax import lax
from jax.experimental import pallas as pl
from jax.experimental.pallas import tpu as pltpu
from jax.sharding import PartitionSpec as P

NB = 100
SEG = 512
SEGS = 12
TILE = 128
QUADS = SEG // TILE
OWN = 64
HALO = 104
REST = HALO - OWN
ROWS = SEGS * 8
PITCH = ROWS + 1
CAP = 1024
UNROLL = 16
JOBS = CAP + UNROLL
BLOCK = 256
VMEM = pl.BlockSpec(memory_space=pltpu.VMEM)
SMEM = pl.BlockSpec(memory_space=pltpu.SMEM)
HBM = pl.BlockSpec(memory_space=pltpu.HBM)


def tables():
    left = np.arange(SEG)[:, None]
    right = np.arange(SEG)[None, :]
    angles = (left * right % (2 * SEG)) * (math.pi / SEG)
    forward = np.concatenate([np.cos(angles), -np.sin(angles)], axis=1) / math.sqrt(SEG)
    angles = (left * (right - SEG // 2) % (2 * SEG)) * (math.pi / SEG)
    weights = np.where(left == 0, 1.0, 2.0) / (math.sqrt(SEG) * SEGS)
    inverse = np.concatenate([weights * np.cos(angles), -weights * np.sin(angles)], axis=0)
    return forward.astype(ml_dtypes.bfloat16), inverse.astype(ml_dtypes.bfloat16)


def spectra(parts, fwd_ref, scaled, loose, spec):
    total = sum(part.shape[1] for part in parts)
    for s in range(SEGS):
        base = s * total
        for part in parts:
            count = part.shape[1]
            tiles = [part[QUADS * s + q].astype(jnp.float32) for q in range(QUADS)]
            squares = sum(tile * tile for tile in tiles)
            power = jnp.sum(squares, axis=1, keepdims=True) * (1.0 / SEG)
            gain = lax.rsqrt(power + 1e-05)
            for q, tile in enumerate(tiles):
                scaled[pl.ds(base, count), q * TILE:(q + 1) * TILE] = (tile * gain).astype(jnp.bfloat16)
            base += count
    for s in range(0, SEGS, 2):
        rows = scaled[pl.ds(s * total, 2 * total), :]
        both = jnp.dot(rows, fwd_ref[...], preferred_element_type=jnp.float32)
        for t in range(2):
            for c in range(2 * QUADS):
                half, g = divmod(c, QUADS)
                row = (half * (SEGS // 2) + s // 2) * 8 + t * QUADS + g
                loose[pl.ds(row, total, stride=PITCH), :] = both[
                    t * total:(t + 1) * total, c * TILE:(c + 1) * TILE]

    def whiten(ch, carry):
        v = [loose[pl.ds(ch * PITCH + r * 8, 8), :] for r in range(SEGS)]
        level = sum(x * x for x in v)
        level = level + pltpu.roll(level, 4, 0)
        gain = lax.rsqrt(level * (1.0 / SEGS) + 0.5)
        for r in range(SEGS):
            spec[pl.ds(pl.multiple_of(ch * ROWS + r * 8, 8), 8), :] = v[r] * gain
        return carry

    lax.fori_loop(0, total, whiten, 0, unroll=4)


def pair_products(order_ref, count, pairs_ref, offset, shift, limit, left_spec, right_spec, cross):
    last = CAP - 1
    low_half = lax.broadcasted_iota(jnp.int32, (8, TILE), 0) < QUADS

    def step(n, carry):
        for t in range(UNROLL):
            p = order_ref[n * UNROLL + t]
            slot = jnp.minimum(p, last)
            i = pl.multiple_of((pairs_ref[0, slot] - offset) * ROWS, 8)
            j = pl.multiple_of(jnp.clip(pairs_ref[1, slot] - (offset + shift), 0, limit) * ROWS, 8)
            row = pl.multiple_of(p * 8, 8)
            real = imag = None
            for h in range(SEGS // 2):
                lr = left_spec[pl.ds(i + h * 8, 8), :]
                li = left_spec[pl.ds(i + (SEGS // 2 + h) * 8, 8), :]
                rr = right_spec[pl.ds(j + h * 8, 8), :]
                ri = right_spec[pl.ds(j + (SEGS // 2 + h) * 8, 8), :]
                if real is None:
                    real = lr * rr + li * ri
                    imag = li * rr - lr * ri
                else:
                    real = real + lr * rr + li * ri
                    imag = imag + li * rr - lr * ri
            real = real + pltpu.roll(real, QUADS, 0)
            imag = imag + pltpu.roll(imag, QUADS, 0)
            cross[pl.ds(row, 8), :] = jnp.where(low_half, real, imag)
        return carry

    lax.fori_loop(0, (count + UNROLL - 1) // UNROLL, step, 0)


def order_kernel(pairs_ref, live_ref, offset_ref, near_ref, far_ref):
    bound = offset_ref[0] + OWN
    live = live_ref[0]

    def step(n, carry):
        near, far = carry
        for t in range(UNROLL):
            p = n * UNROLL + t
            inside = (pairs_ref[1, p] < bound).astype(jnp.int32)
            near_ref[near] = p
            far_ref[far] = p
            near = near + inside
            far = far + 1 - inside
        return near, far

    blocks = live // UNROLL
    near, far = lax.fori_loop(0, blocks, step, (jnp.int32(0), jnp.int32(0)))

    def single(p, carry):
        near, far = carry
        inside = (pairs_ref[1, p] < bound).astype(jnp.int32)
        near_ref[near] = p
        far_ref[far] = p
        return near + inside, far + 1 - inside

    near, far = lax.fori_loop(blocks * UNROLL, live, single, (near, far))
    for ref, count in ((near_ref, near), (far_ref, far)):
        for t in range(UNROLL):
            ref[count + t] = CAP
        ref[JOBS] = count
        ref[JOBS + 1] = live
        ref[JOBS + 2] = offset_ref[0]


def near_kernel(order_ref, pairs_ref, own_ref, fwd_ref, kept, scaled, loose, spec, cross, sems):
    spectra([own_ref], fwd_ref, scaled, loose, spec)
    spec_copy = pltpu.make_async_copy(spec, kept.at[pl.ds(0, OWN * ROWS), :], sems.at[0])
    spec_copy.start()
    pair_products(order_ref, order_ref[JOBS], pairs_ref, order_ref[JOBS + 2], 0, OWN - 1, spec, spec, cross)
    cross_copy = pltpu.make_async_copy(cross, kept.at[pl.ds(OWN * ROWS, CROSS[0]), :], sems.at[1])
    cross_copy.start()
    spec_copy.wait()
    cross_copy.wait()


def far_kernel(order_ref, pairs_ref, h1_ref, h2_ref, kept, fwd_ref, inv_ref, out_ref,
               scaled, loose, halo, spec, cross, stacks, sems):
    spec_copy = pltpu.make_async_copy(kept.at[pl.ds(0, OWN * ROWS), :], spec, sems.at[0])
    cross_copy = pltpu.make_async_copy(kept.at[pl.ds(OWN * ROWS, CROSS[0]), :], cross, sems.at[1])
    spec_copy.start()
    cross_copy.start()
    spectra([h1_ref, h2_ref], fwd_ref, scaled, loose, halo)
    spec_copy.wait()
    cross_copy.wait()
    pair_products(order_ref, order_ref[JOBS], pairs_ref, order_ref[JOBS + 2], OWN, HALO - 1, spec, halo, cross)
    live = order_ref[JOBS + 1]
    copies = []
    for b in range(CAP // BLOCK):
        rows = pl.ds(b * BLOCK, BLOCK)

        @pl.when(b * BLOCK < live)
        def _():
            columns = [cross[pl.ds(b * BLOCK * 8 + g, BLOCK, stride=8), :].astype(jnp.bfloat16) for g in range(8)]
            lagged = jnp.dot(
                jnp.concatenate(columns, axis=1), inv_ref[...], preferred_element_type=jnp.float32)
            slot = lax.broadcasted_iota(jnp.int32, (BLOCK, SEG), 0) + b * BLOCK
            stacks[rows, :] = jnp.where(slot < live, lagged, 0.0)

        @pl.when(b * BLOCK >= live)
        def _():
            stacks[rows, :] = jnp.zeros((BLOCK, SEG), jnp.float32)

        copies.append(pltpu.make_async_copy(stacks.at[rows, :], out_ref.at[rows, :], sems.at[2 + b]))
        copies[-1].start()
    for copy in copies:
        copy.wait()


def ints(*shape):
    return jax.ShapeDtypeStruct(shape, jnp.int32)


def floats(*shape):
    return jax.ShapeDtypeStruct(shape, jnp.float32)


CROSS = ((CAP + 1) * 8, TILE)


def order_pairs(pair_list, live, offset):
    return pl.pallas_call(
        order_kernel,
        out_shape=(ints(JOBS + 16), ints(JOBS + 16)),
        in_specs=[SMEM] * 3,
        out_specs=(SMEM,) * 2,
        name="order_pairs",
    )(pair_list, live, offset)


def near_pairs(order, pair_list, own, fwd):
    return pl.pallas_call(
        near_kernel,
        out_shape=floats(OWN * ROWS + CROSS[0], TILE),
        in_specs=[SMEM, SMEM, VMEM, VMEM],
        out_specs=HBM,
        scratch_shapes=[
            pltpu.VMEM((SEGS * OWN, SEG), jnp.bfloat16),
            pltpu.VMEM((OWN * PITCH + 8, TILE), jnp.float32),
            pltpu.VMEM((OWN * ROWS, TILE), jnp.float32),
            pltpu.VMEM(CROSS, jnp.float32),
            pltpu.SemaphoreType.DMA((2,)),
        ],
        compiler_params=pltpu.CompilerParams(vmem_limit_bytes=50 << 20),
        name="near_pairs",
    )(order, pair_list, own, fwd)


def far_pairs(order, pair_list, h1, h2, kept, fwd, inv):
    return pl.pallas_call(
        far_kernel,
        out_shape=floats(CAP, SEG),
        in_specs=[SMEM, SMEM, VMEM, VMEM, HBM, VMEM, VMEM],
        out_specs=HBM,
        scratch_shapes=[
            pltpu.VMEM((SEGS * HALO, SEG), jnp.bfloat16),
            pltpu.VMEM((HALO * PITCH + 8, TILE), jnp.float32),
            pltpu.VMEM((HALO * ROWS, TILE), jnp.float32),
            pltpu.VMEM((OWN * ROWS, TILE), jnp.float32),
            pltpu.VMEM(CROSS, jnp.float32),
            pltpu.VMEM((CAP, SEG), jnp.float32),
            pltpu.SemaphoreType.DMA((2 + CAP // BLOCK,)),
        ],
        compiler_params=pltpu.CompilerParams(vmem_limit_bytes=50 << 20),
        name="far_pairs",
    )(order, pair_list, h1, h2, kept, fwd, inv)


def turn_kernel(panels, part, whole, sems):
    copies = []
    for turned in (part, whole):
        count = turned.shape[2]
        for a in range(panels.shape[0]):
            source = panels.at[a, :, pl.ds(0, count), :]
            copies.append(pltpu.make_async_copy(source, turned.at[:, a], sems.at[len(copies)]))
    for copy in copies:
        copy.start()
    for copy in copies:
        copy.wait()


def turn(panels):
    tiles, sections, _, width = panels.shape
    return pl.pallas_call(
        turn_kernel,
        out_shape=[
            jax.ShapeDtypeStruct((sections, tiles, count, width), panels.dtype) for count in (REST, OWN)],
        in_specs=[HBM],
        out_specs=[HBM] * 2,
        scratch_shapes=[pltpu.SemaphoreType.DMA((2 * tiles,))],
        compiler_params=pltpu.CompilerParams(vmem_limit_bytes=60<<20),
        name="turn",
    )(panels)


def from_ahead(block, axis, distance):
    devices = range(lax.axis_size(axis))
    route = [(i + distance, i) for i in devices if i + distance in devices]
    return lax.ppermute(block, axis, route)


def by_section(block):
    rows = lax.all_to_all(block, "tm", split_axis=0, concat_axis=0, tiled=True)
    return rows.reshape(-1, *block.shape[2:])


def per_device(panels, pair_list, pair_count):
    fwd, inv = (jnp.asarray(table) for table in tables())
    offset = (lax.axis_index("tm") * lax.axis_size("pairs") + lax.axis_index("pairs")) * OWN
    near, far = order_pairs(pair_list, pair_count, offset.astype(jnp.int32)[None])
    part, whole = turn(panels)
    h2_turned = from_ahead(part, "pairs", 2)
    own = by_section(whole)
    h2 = by_section(h2_turned)
    own, near, far = lax.optimization_barrier((own, near, far))
    h1 = from_ahead(own, "pairs", 1)
    kept = near_pairs(near, pair_list, own, fwd)
    return far_pairs(far, pair_list, h1, h2, kept, fwd, inv)


def solution(mesh):
    return jax.shard_map(
        per_device,
        mesh=mesh,
        in_specs=(P("tm", None, "pairs", None), P(None, ("tm", "pairs")), P(("tm", "pairs"))),
        out_specs=P(("tm", "pairs"), None),
        check_vma=False,
    )
```

```python
import math

import jax
import jax.numpy as jnp
import ml_dtypes
import numpy as np
from jax import lax
from jax.experimental import pallas as pl
from jax.experimental.pallas import tpu as pltpu
from jax.sharding import PartitionSpec as P

NB = 100
SEG = 512
SEGS = 12
TILE = 128
QUADS = SEG // TILE
OWN = 64
HALO = 104
REST = HALO - OWN
ROWS = SEGS * 8
PITCH = ROWS + 1
CAP = 1024
UNROLL = 32
LIMIT = 50 << 20
BLOCK = 256
VMEM = pl.BlockSpec(memory_space=pltpu.VMEM)
SMEM = pl.BlockSpec(memory_space=pltpu.SMEM)
HBM = pl.BlockSpec(memory_space=pltpu.HBM)


def tables():
    left = np.arange(SEG)[:, None]
    right = np.arange(SEG)[None, :]
    angles = (left * right % (2 * SEG)) * (math.pi / SEG)
    forward = np.concatenate([np.cos(angles), -np.sin(angles)], axis=1) / math.sqrt(SEG)
    angles = (left * (right - SEG // 2) % (2 * SEG)) * (math.pi / SEG)
    weights = np.where(left == 0, 1.0, 2.0) / (math.sqrt(SEG) * SEGS)
    inverse = np.concatenate([weights * np.cos(angles), -weights * np.sin(angles)], axis=0)
    return forward.astype(ml_dtypes.bfloat16), inverse.astype(ml_dtypes.bfloat16)


def spectra(parts, fwd_ref, scaled, loose, spec, first):
    total = sum(part.shape[1] for part in parts)
    for s in range(SEGS):
        base = s * total
        for part in parts:
            count = part.shape[1]
            tiles = [part[QUADS * s + q].astype(jnp.float32) for q in range(QUADS)]
            squares = sum(tile * tile for tile in tiles)
            power = jnp.sum(squares, axis=1, keepdims=True) * (1.0 / SEG)
            gain = lax.rsqrt(power + 1e-05)
            for q, tile in enumerate(tiles):
                scaled[pl.ds(base, count), q * TILE:(q + 1) * TILE] = (tile * gain).astype(jnp.bfloat16)
            base += count
    for s in range(0, SEGS, 2):
        rows = scaled[pl.ds(s * total, 2 * total), :]
        both = jnp.dot(rows, fwd_ref[...], preferred_element_type=jnp.float32)
        for t in range(2):
            for c in range(2 * QUADS):
                half, g = divmod(c, QUADS)
                row = (half * (SEGS // 2) + s // 2) * 8 + t * QUADS + g
                loose[pl.ds(row, total, stride=PITCH), :] = both[
                    t * total:(t + 1) * total, c * TILE:(c + 1) * TILE]

    def whiten(ch, carry):
        v = [loose[pl.ds(ch * PITCH + r * 8, 8), :] for r in range(SEGS)]
        level = sum(x * x for x in v)
        level = level + pltpu.roll(level, 4, 0)
        gain = lax.rsqrt(level * (1.0 / SEGS) + 0.5)
        for r in range(SEGS):
            spec[pl.ds(pl.multiple_of((first + ch) * ROWS + r * 8, 8), 8), :] = v[r] * gain
        return carry

    lax.fori_loop(0, total, whiten, 0, unroll=4)


def pair_products(count, idx_ref, spec, cross):
    low_half = lax.broadcasted_iota(jnp.int32, (8, TILE), 0) < QUADS

    def step(n, carry):
        for t in range(UNROLL):
            p = n * UNROLL + t
            i = pl.multiple_of(idx_ref[0, p], 8)
            j = pl.multiple_of(idx_ref[1, p], 8)
            real = imag = None
            for h in range(SEGS // 2):
                lr = spec[pl.ds(i + h * 8, 8), :]
                li = spec[pl.ds(i + (SEGS // 2 + h) * 8, 8), :]
                rr = spec[pl.ds(j + h * 8, 8), :]
                ri = spec[pl.ds(j + (SEGS // 2 + h) * 8, 8), :]
                if real is None:
                    real = lr * rr + li * ri
                    imag = li * rr - lr * ri
                else:
                    real = real + lr * rr + li * ri
                    imag = imag + li * rr - lr * ri
            real = real + pltpu.roll(real, QUADS, 0)
            imag = imag + pltpu.roll(imag, QUADS, 0)
            cross[pl.ds(pl.multiple_of(p * 8, 8), 8), :] = jnp.where(low_half, real, imag)
        return carry

    lax.fori_loop(0, (count + UNROLL - 1) // UNROLL, step, 0)


def own_kernel(own_ref, fwd_ref, kept, scaled, loose, spec, sem):
    spectra([own_ref], fwd_ref, scaled, loose, spec, 0)
    copy = pltpu.make_async_copy(spec, kept, sem)
    copy.start()
    copy.wait()


def pair_kernel(idx_ref, live_ref, h1_ref, h2_ref, kept, fwd_ref, inv_ref, out_ref,
                scaled, loose, spec, cross, stacks, sems):
    kept_copy = pltpu.make_async_copy(kept, spec.at[pl.ds(0, OWN * ROWS), :], sems.at[0])
    kept_copy.start()
    spectra([h1_ref, h2_ref], fwd_ref, scaled, loose, spec, OWN)
    kept_copy.wait()
    live = live_ref[0]
    pair_products(live, idx_ref, spec, cross)
    copies = []
    for b in range(CAP // BLOCK):
        rows = pl.ds(b * BLOCK, BLOCK)

        @pl.when(b * BLOCK < live)
        def _():
            columns = [cross[pl.ds(b * BLOCK * 8 + g, BLOCK, stride=8), :].astype(jnp.bfloat16) for g in range(8)]
            lagged = jnp.dot(
                jnp.concatenate(columns, axis=1), inv_ref[...], preferred_element_type=jnp.float32)
            slot = lax.broadcasted_iota(jnp.int32, (BLOCK, SEG), 0) + b * BLOCK
            stacks[rows, :] = jnp.where(slot < live, lagged, 0.0)

        @pl.when(b * BLOCK >= live)
        def _():
            stacks[rows, :] = jnp.zeros((BLOCK, SEG), jnp.float32)

        copies.append(pltpu.make_async_copy(stacks.at[rows, :], out_ref.at[rows, :], sems.at[1 + b]))
        copies[-1].start()
    for copy in copies:
        copy.wait()


def floats(*shape):
    return jax.ShapeDtypeStruct(shape, jnp.float32)


def own_spectra(own, fwd):
    return pl.pallas_call(
        own_kernel,
        out_shape=floats(OWN * ROWS, TILE),
        in_specs=[VMEM, VMEM],
        out_specs=HBM,
        scratch_shapes=[
            pltpu.VMEM((SEGS * OWN, SEG), jnp.bfloat16),
            pltpu.VMEM((OWN * PITCH + 8, TILE), jnp.float32),
            pltpu.VMEM((OWN * ROWS, TILE), jnp.float32),
            pltpu.SemaphoreType.DMA(()),
        ],
        compiler_params=pltpu.CompilerParams(vmem_limit_bytes=LIMIT),
        name="own_spectra",
    )(own, fwd)


def pair_stacks(idx, live, h1, h2, kept, fwd, inv):
    return pl.pallas_call(
        pair_kernel,
        out_shape=floats(CAP, SEG),
        in_specs=[SMEM, SMEM, VMEM, VMEM, HBM, VMEM, VMEM],
        out_specs=HBM,
        scratch_shapes=[
            pltpu.VMEM((SEGS * HALO, SEG), jnp.bfloat16),
            pltpu.VMEM((HALO * PITCH + 8, TILE), jnp.float32),
            pltpu.VMEM(((OWN + HALO) * ROWS, TILE), jnp.float32),
            pltpu.VMEM((CAP * 8, TILE), jnp.float32),
            pltpu.VMEM((CAP, SEG), jnp.float32),
            pltpu.SemaphoreType.DMA((1 + CAP // BLOCK,)),
        ],
        compiler_params=pltpu.CompilerParams(vmem_limit_bytes=LIMIT),
        name="pair_stacks",
    )(idx, live, h1, h2, kept, fwd, inv)


def from_ahead(block, axis, distance):
    devices = range(lax.axis_size(axis))
    route = [(i + distance, i) for i in devices if i + distance in devices]
    return lax.ppermute(block, axis, route)


def by_section(block):
    rows = lax.all_to_all(block, "tm", split_axis=0, concat_axis=0, tiled=True)
    return rows.reshape(-1, *block.shape[2:])


def per_device(panels, pair_list, pair_count):
    fwd, inv = (jnp.asarray(table) for table in tables())
    offset = (lax.axis_index("tm") * lax.axis_size("pairs") + lax.axis_index("pairs")) * OWN
    idx = (pair_list - offset) * ROWS
    turned = jnp.transpose(panels, (1, 0, 2, 3))
    h2_turned = from_ahead(turned[:, :, :REST], "pairs", 2)
    own = by_section(turned)
    h1 = from_ahead(own, "pairs", 1)
    h2 = by_section(h2_turned)
    kept = own_spectra(own, fwd)
    return pair_stacks(idx, pair_count, h1, h2, kept, fwd, inv)


def solution(mesh):
    return jax.shard_map(
        per_device,
        mesh=mesh,
        in_specs=(P("tm", None, "pairs", None), P(None, ("tm", "pairs")), P(("tm", "pairs"))),
        out_specs=P(("tm", "pairs"), None),
        check_vma=False,
    )
```

```python
import math

import jax
import jax.numpy as jnp
import ml_dtypes
import numpy as np
from jax import lax
from jax.experimental import pallas as pl
from jax.experimental.pallas import tpu as pltpu
from jax.sharding import PartitionSpec as P

NB = 100
SEG = 512
SEGS = 12
TILE = 128
QUADS = SEG // TILE
OWN = 64
HALO = 104
REST = HALO - OWN
ROWS = SEGS * 8
PITCH = ROWS + 1
CAP = 1024
UNROLL = 32
LIMIT = 50 << 20
BLOCK = 256
VMEM = pl.BlockSpec(memory_space=pltpu.VMEM)
SMEM = pl.BlockSpec(memory_space=pltpu.SMEM)
HBM = pl.BlockSpec(memory_space=pltpu.HBM)


def tables():
    left = np.arange(SEG)[:, None]
    right = np.arange(SEG)[None, :]
    angles = (left * right % (2 * SEG)) * (math.pi / SEG)
    forward = np.concatenate([np.cos(angles), -np.sin(angles)], axis=1) / math.sqrt(SEG)
    angles = (left * (right - SEG // 2) % (2 * SEG)) * (math.pi / SEG)
    weights = np.where(left == 0, 1.0, 2.0) / (math.sqrt(SEG) * SEGS)
    inverse = np.concatenate([weights * np.cos(angles), -weights * np.sin(angles)], axis=0)
    return forward.astype(ml_dtypes.bfloat16), inverse.astype(ml_dtypes.bfloat16)


def aligned(rows):
    return -(-rows // 16) * 16


def spectra(parts, fwd_ref, scaled, loose, spec, first):
    total = sum(part.shape[1] for part in parts)
    pitch = aligned(total)
    for s in range(SEGS):
        base = s * pitch
        for part in parts:
            count = part.shape[1]
            tiles = [part[QUADS * s + q].astype(jnp.float32) for q in range(QUADS)]
            squares = sum(tile * tile for tile in tiles)
            power = jnp.sum(squares, axis=1, keepdims=True) * (1.0 / SEG)
            gain = lax.rsqrt(power + 1e-05)
            for q, tile in enumerate(tiles):
                scaled[pl.ds(base, count), q * TILE:(q + 1) * TILE] = (tile * gain).astype(jnp.bfloat16)
            base += count
    for s in range(0, SEGS, 2):
        rows = scaled[pl.ds(s * pitch, 2 * pitch), :]
        both = jnp.dot(rows, fwd_ref[...], preferred_element_type=jnp.float32)
        for t in range(2):
            for c in range(2 * QUADS):
                half, g = divmod(c, QUADS)
                row = (half * (SEGS // 2) + s // 2) * 8 + t * QUADS + g
                loose[pl.ds(row, total, stride=PITCH), :] = both[
                    t * pitch:t * pitch + total, c * TILE:(c + 1) * TILE]

    def whiten(ch, carry):
        v = [loose[pl.ds(ch * PITCH + r * 8, 8), :] for r in range(SEGS)]
        level = sum(x * x for x in v)
        level = level + pltpu.roll(level, 4, 0)
        gain = lax.rsqrt(level * (1.0 / SEGS) + 0.5)
        for r in range(SEGS):
            spec[pl.ds(pl.multiple_of((first + ch) * ROWS + r * 8, 8), 8), :] = v[r] * gain
        return carry

    lax.fori_loop(0, total, whiten, 0, unroll=4)


def pair_products(count, idx_ref, spec, cross):
    low_half = lax.broadcasted_iota(jnp.int32, (8, TILE), 0) < QUADS

    def step(n, carry):
        for t in range(UNROLL):
            p = n * UNROLL + t
            i = pl.multiple_of(idx_ref[0, p], 8)
            j = pl.multiple_of(idx_ref[1, p], 8)
            real = imag = None
            for h in range(SEGS // 2):
                lr = spec[pl.ds(i + h * 8, 8), :]
                li = spec[pl.ds(i + (SEGS // 2 + h) * 8, 8), :]
                rr = spec[pl.ds(j + h * 8, 8), :]
                ri = spec[pl.ds(j + (SEGS // 2 + h) * 8, 8), :]
                if real is None:
                    real = lr * rr + li * ri
                    imag = li * rr - lr * ri
                else:
                    real = real + lr * rr + li * ri
                    imag = imag + li * rr - lr * ri
            real = real + pltpu.roll(real, QUADS, 0)
            imag = imag + pltpu.roll(imag, QUADS, 0)
            cross[pl.ds(pl.multiple_of(p * 8, 8), 8), :] = jnp.where(low_half, real, imag)
        return carry

    lax.fori_loop(0, (count + UNROLL - 1) // UNROLL, step, 0)


def own_kernel(own_ref, fwd_ref, kept, scaled, loose, spec, sem):
    spectra([own_ref], fwd_ref, scaled, loose, spec, 0)
    copy = pltpu.make_async_copy(spec, kept, sem)
    copy.start()
    copy.wait()


def pair_kernel(idx_ref, live_ref, h1_ref, h2_ref, kept, fwd_ref, inv_ref, out_ref,
                scaled, loose, spec, cross, stacks, sems):
    kept_copy = pltpu.make_async_copy(kept, spec.at[pl.ds(0, OWN * ROWS), :], sems.at[0])
    kept_copy.start()
    spectra([h1_ref, h2_ref], fwd_ref, scaled, loose, spec, OWN)
    kept_copy.wait()
    live = live_ref[0]
    pair_products(live, idx_ref, spec, cross)
    copies = []
    for b in range(CAP // BLOCK):
        rows = pl.ds(b * BLOCK, BLOCK)

        @pl.when(b * BLOCK < live)
        def _():
            columns = [cross[pl.ds(b * BLOCK * 8 + g, BLOCK, stride=8), :].astype(jnp.bfloat16) for g in range(8)]
            lagged = jnp.dot(
                jnp.concatenate(columns, axis=1), inv_ref[...], preferred_element_type=jnp.float32)
            slot = lax.broadcasted_iota(jnp.int32, (BLOCK, SEG), 0) + b * BLOCK
            stacks[rows, :] = jnp.where(slot < live, lagged, 0.0)

        @pl.when(b * BLOCK >= live)
        def _():
            stacks[rows, :] = jnp.zeros((BLOCK, SEG), jnp.float32)

        copies.append(pltpu.make_async_copy(stacks.at[rows, :], out_ref.at[rows, :], sems.at[1 + b]))
        copies[-1].start()
    for copy in copies:
        copy.wait()


def floats(*shape):
    return jax.ShapeDtypeStruct(shape, jnp.float32)


def own_spectra(own, fwd):
    return pl.pallas_call(
        own_kernel,
        out_shape=floats(OWN * ROWS, TILE),
        in_specs=[VMEM, VMEM],
        out_specs=HBM,
        scratch_shapes=[
            pltpu.VMEM((SEGS * OWN, SEG), jnp.bfloat16),
            pltpu.VMEM((OWN * PITCH + 8, TILE), jnp.float32),
            pltpu.VMEM((OWN * ROWS, TILE), jnp.float32),
            pltpu.SemaphoreType.DMA(()),
        ],
        compiler_params=pltpu.CompilerParams(vmem_limit_bytes=LIMIT),
        name="own_spectra",
    )(own, fwd)


def pair_stacks(idx, live, h1, h2, kept, fwd, inv):
    return pl.pallas_call(
        pair_kernel,
        out_shape=floats(CAP, SEG),
        in_specs=[SMEM, SMEM, VMEM, VMEM, HBM, VMEM, VMEM],
        out_specs=HBM,
        scratch_shapes=[
            pltpu.VMEM((SEGS * aligned(HALO), SEG), jnp.bfloat16),
            pltpu.VMEM((HALO * PITCH + 8, TILE), jnp.float32),
            pltpu.VMEM(((OWN + HALO) * ROWS, TILE), jnp.float32),
            pltpu.VMEM((CAP * 8, TILE), jnp.float32),
            pltpu.VMEM((CAP, SEG), jnp.float32),
            pltpu.SemaphoreType.DMA((1 + CAP // BLOCK,)),
        ],
        compiler_params=pltpu.CompilerParams(vmem_limit_bytes=LIMIT),
        name="pair_stacks",
    )(idx, live, h1, h2, kept, fwd, inv)


def turn_kernel(panels, part, whole, sems):
    copies = []
    for turned in (part, whole):
        count = turned.shape[2]
        for a in range(panels.shape[0]):
            source = panels.at[a, :, pl.ds(0, count), :]
            copies.append(pltpu.make_async_copy(source, turned.at[:, a], sems.at[len(copies)]))
            copies[-1].start()
    for copy in copies:
        copy.wait()


def turn(panels):
    tiles, sections, _, width = panels.shape
    return pl.pallas_call(
        turn_kernel,
        out_shape=[
            jax.ShapeDtypeStruct((sections, tiles, count, width), panels.dtype) for count in (REST, OWN)],
        in_specs=[VMEM],
        out_specs=[HBM] * 2,
        scratch_shapes=[pltpu.SemaphoreType.DMA((2 * tiles,))],
        compiler_params=pltpu.CompilerParams(vmem_limit_bytes=LIMIT),
        name="turn",
    )(panels)


def from_ahead(block, axis, distance):
    devices = range(lax.axis_size(axis))
    route = [(i + distance, i) for i in devices if i + distance in devices]
    return lax.ppermute(block, axis, route)


def by_section(block):
    rows = lax.all_to_all(block, "tm", split_axis=0, concat_axis=0, tiled=True)
    return rows.reshape(-1, *block.shape[2:])


def per_device(panels, pair_list, pair_count):
    fwd, inv = (jnp.asarray(table) for table in tables())
    offset = (lax.axis_index("tm") * lax.axis_size("pairs") + lax.axis_index("pairs")) * OWN
    idx = (pair_list - offset) * ROWS
    part, whole = turn(panels)
    h2_turned = from_ahead(part, "pairs", 2)
    own = by_section(whole)
    h1 = from_ahead(own, "pairs", 1)
    h2 = by_section(h2_turned)
    kept = own_spectra(own, fwd)
    return pair_stacks(idx, pair_count, h1, h2, kept, fwd, inv)


def solution(mesh):
    return jax.shard_map(
        per_device,
        mesh=mesh,
        in_specs=(P("tm", None, "pairs", None), P(None, ("tm", "pairs")), P(("tm", "pairs"))),
        out_specs=P(("tm", "pairs"), None),
        check_vma=False,
    )
```

```python
import math

import jax
import jax.numpy as jnp
import ml_dtypes
import numpy as np
from jax import lax
from jax.experimental import pallas as pl
from jax.experimental.pallas import tpu as pltpu
from jax.sharding import PartitionSpec as P

NB = 100
SEG = 512
SEGS = 12
TILE = 128
QUADS = SEG // TILE
OWN = 64
HALO = 104
REST = HALO - OWN
ROWS = SEGS * 8
PITCH = ROWS + 1
CAP = 1024
UNROLL = 32
LIMIT = 28 << 20
BLOCK = 256
VMEM = pl.BlockSpec(memory_space=pltpu.VMEM)
SMEM = pl.BlockSpec(memory_space=pltpu.SMEM)
HBM = pl.BlockSpec(memory_space=pltpu.HBM)


def tables():
    left = np.arange(SEG)[:, None]
    right = np.arange(SEG)[None, :]
    angles = (left * right % (2 * SEG)) * (math.pi / SEG)
    forward = np.concatenate([np.cos(angles), -np.sin(angles)], axis=1) / math.sqrt(SEG)
    angles = (left * (right - SEG // 2) % (2 * SEG)) * (math.pi / SEG)
    weights = np.where(left == 0, 1.0, 2.0) / (math.sqrt(SEG) * SEGS)
    inverse = np.concatenate([weights * np.cos(angles), -weights * np.sin(angles)], axis=0)
    return forward.astype(ml_dtypes.bfloat16), inverse.astype(ml_dtypes.bfloat16)


def aligned(rows):
    return -(-rows // 16) * 16


def spectra(parts, fwd_ref, scaled, loose, spec, first):
    total = sum(part.shape[1] for part in parts)
    pitch = aligned(total)
    for s in range(SEGS):
        base = s * pitch
        for part in parts:
            count = part.shape[1]
            tiles = [part[QUADS * s + q].astype(jnp.float32) for q in range(QUADS)]
            squares = sum(tile * tile for tile in tiles)
            power = jnp.sum(squares, axis=1, keepdims=True) * (1.0 / SEG)
            gain = lax.rsqrt(power + 1e-05)
            for q, tile in enumerate(tiles):
                scaled[pl.ds(base, count), q * TILE:(q + 1) * TILE] = (tile * gain).astype(jnp.bfloat16)
            base += count
    for s in range(0, SEGS, 2):
        rows = scaled[pl.ds(s * pitch, 2 * pitch), :]
        both = jnp.dot(rows, fwd_ref[...], preferred_element_type=jnp.float32)
        for t in range(2):
            for c in range(2 * QUADS):
                half, g = divmod(c, QUADS)
                row = (half * (SEGS // 2) + s // 2) * 8 + t * QUADS + g
                loose[pl.ds(row, total, stride=PITCH), :] = both[
                    t * pitch:t * pitch + total, c * TILE:(c + 1) * TILE]

    def whiten(ch, carry):
        v = [loose[pl.ds(ch * PITCH + r * 8, 8), :] for r in range(SEGS)]
        level = sum(x * x for x in v)
        level = level + pltpu.roll(level, 4, 0)
        gain = lax.rsqrt(level * (1.0 / SEGS) + 0.5)
        for r in range(SEGS):
            spec[pl.ds(pl.multiple_of((first + ch) * ROWS + r * 8, 8), 8), :] = v[r] * gain
        return carry

    lax.fori_loop(0, total, whiten, 0, unroll=4)


def pair_products(count, idx_ref, spec, cross):
    low_half = lax.broadcasted_iota(jnp.int32, (8, TILE), 0) < QUADS

    def step(n, carry):
        for t in range(UNROLL):
            p = n * UNROLL + t
            i = pl.multiple_of(idx_ref[0, p], 8)
            j = pl.multiple_of(idx_ref[1, p], 8)
            real = imag = None
            for h in range(SEGS // 2):
                lr = spec[pl.ds(i + h * 8, 8), :]
                li = spec[pl.ds(i + (SEGS // 2 + h) * 8, 8), :]
                rr = spec[pl.ds(j + h * 8, 8), :]
                ri = spec[pl.ds(j + (SEGS // 2 + h) * 8, 8), :]
                if real is None:
                    real = lr * rr + li * ri
                    imag = li * rr - lr * ri
                else:
                    real = real + lr * rr + li * ri
                    imag = imag + li * rr - lr * ri
            real = real + pltpu.roll(real, QUADS, 0)
            imag = imag + pltpu.roll(imag, QUADS, 0)
            cross[pl.ds(pl.multiple_of(p * 8, 8), 8), :] = jnp.where(low_half, real, imag)
        return carry

    lax.fori_loop(0, (count + UNROLL - 1) // UNROLL, step, 0)


def early_kernel(own_ref, h2_ref, fwd_ref, spec, scaled, loose):
    spectra([own_ref, h2_ref], fwd_ref, scaled, loose, spec, 0)


def pair_kernel(idx_ref, live_ref, h1_ref, early, fwd_ref, inv_ref, out_ref, spec,
                scaled, loose, cross, stacks, sems):
    spectra([h1_ref], fwd_ref, scaled, loose, spec, OWN + REST)
    live = live_ref[0]
    pair_products(live, idx_ref, spec, cross)
    copies = []
    for b in range(CAP // BLOCK):
        rows = pl.ds(b * BLOCK, BLOCK)

        @pl.when(b * BLOCK < live)
        def _():
            columns = [cross[pl.ds(b * BLOCK * 8 + g, BLOCK, stride=8), :].astype(jnp.bfloat16) for g in range(8)]
            lagged = jnp.dot(
                jnp.concatenate(columns, axis=1), inv_ref[...], preferred_element_type=jnp.float32)
            slot = lax.broadcasted_iota(jnp.int32, (BLOCK, SEG), 0) + b * BLOCK
            stacks[rows, :] = jnp.where(slot < live, lagged, 0.0)

        @pl.when(b * BLOCK >= live)
        def _():
            stacks[rows, :] = jnp.zeros((BLOCK, SEG), jnp.float32)

        copies.append(pltpu.make_async_copy(stacks.at[rows, :], out_ref.at[rows, :], sems.at[b]))
        copies[-1].start()
    for copy in copies:
        copy.wait()


def floats(*shape):
    return jax.ShapeDtypeStruct(shape, jnp.float32)


def spectra_scratch(count):
    return [
        pltpu.VMEM((SEGS * aligned(count), SEG), jnp.bfloat16),
        pltpu.VMEM((count * PITCH + 8, TILE), jnp.float32),
    ]


def early_spectra(own, h2, fwd):
    return pl.pallas_call(
        early_kernel,
        out_shape=floats((OWN + HALO) * ROWS, TILE),
        in_specs=[VMEM] * 3,
        out_specs=VMEM,
        scratch_shapes=spectra_scratch(OWN + REST),
        compiler_params=pltpu.CompilerParams(vmem_limit_bytes=LIMIT),
        cost_estimate=pl.CostEstimate(flops=3 * 10**10, transcendentals=0, bytes_accessed=10**8),
        name="early_spectra",
    )(own, h2, fwd)


def pair_stacks(idx, live, h1, early, fwd, inv):
    return pl.pallas_call(
        pair_kernel,
        out_shape=[floats(CAP, SEG), floats((OWN + HALO) * ROWS, TILE)],
        in_specs=[SMEM, SMEM, VMEM, VMEM, VMEM, VMEM],
        out_specs=[HBM, VMEM],
        input_output_aliases={3: 1},
        scratch_shapes=spectra_scratch(OWN) + [
            pltpu.VMEM((CAP * 8, TILE), jnp.float32),
            pltpu.VMEM((CAP, SEG), jnp.float32),
            pltpu.SemaphoreType.DMA((CAP // BLOCK,)),
        ],
        compiler_params=pltpu.CompilerParams(vmem_limit_bytes=LIMIT),
        name="pair_stacks",
    )(idx, live, h1, early, fwd, inv)[0]


def turn_kernel(panels, part, whole, sems):
    copies = []
    for turned in (part, whole):
        count = turned.shape[2]
        for a in range(panels.shape[0]):
            source = panels.at[a, :, pl.ds(0, count), :]
            copies.append(pltpu.make_async_copy(source, turned.at[:, a], sems.at[len(copies)]))
            copies[-1].start()
    for copy in copies:
        copy.wait()


def turn(panels):
    tiles, sections, _, width = panels.shape
    return pl.pallas_call(
        turn_kernel,
        out_shape=[
            jax.ShapeDtypeStruct((sections, tiles, count, width), panels.dtype) for count in (REST, OWN)],
        in_specs=[VMEM],
        out_specs=[HBM] * 2,
        scratch_shapes=[pltpu.SemaphoreType.DMA((2 * tiles,))],
        compiler_params=pltpu.CompilerParams(vmem_limit_bytes=LIMIT),
        name="turn",
    )(panels)


def from_ahead(block, axis, distance):
    devices = range(lax.axis_size(axis))
    route = [(i + distance, i) for i in devices if i + distance in devices]
    return lax.ppermute(block, axis, route)


def by_section(block):
    rows = lax.all_to_all(block, "tm", split_axis=0, concat_axis=0, tiled=True)
    return rows.reshape(-1, *block.shape[2:])


def per_device(panels, pair_list, pair_count):
    fwd, inv = (jnp.asarray(table) for table in tables())
    offset = (lax.axis_index("tm") * lax.axis_size("pairs") + lax.axis_index("pairs")) * OWN
    place = pair_list - offset
    place = jnp.where(place < OWN, place, jnp.where(place < 2 * OWN, place + REST, place - OWN))
    part, whole = turn(panels)
    h2_turned = from_ahead(part, "pairs", 2)
    own = by_section(whole)
    own, h2_turned = lax.optimization_barrier((own, h2_turned))
    h2 = by_section(h2_turned)
    h1 = from_ahead(own, "pairs", 1)
    early = early_spectra(own, h2, fwd)
    return pair_stacks(place * ROWS, pair_count, h1, early, fwd, inv)


def solution(mesh):
    return jax.shard_map(
        per_device,
        mesh=mesh,
        in_specs=(P("tm", None, "pairs", None), P(None, ("tm", "pairs")), P(("tm", "pairs"))),
        out_specs=P(("tm", "pairs"), None),
        check_vma=False,
    )
```

```python
import math

import jax
import jax.numpy as jnp
import ml_dtypes
import numpy as np
from jax import lax
from jax.experimental import pallas as pl
from jax.experimental.pallas import tpu as pltpu
from jax.sharding import PartitionSpec as P

NB = 100
SEG = 512
SEGS = 12
TILE = 128
QUADS = SEG // TILE
OWN = 64
HALO = 104
REST = HALO - OWN
ROWS = SEGS * 8
PITCH = ROWS + 1
CAP = 1024
UNROLL = 32
LIMIT = 50 << 20
TURNS = 2
BLOCK = 256
VMEM = pl.BlockSpec(memory_space=pltpu.VMEM)
SMEM = pl.BlockSpec(memory_space=pltpu.SMEM)
HBM = pl.BlockSpec(memory_space=pltpu.HBM)


def tables():
    left = np.arange(SEG)[:, None]
    right = np.arange(SEG)[None, :]
    angles = (left * right % (2 * SEG)) * (math.pi / SEG)
    forward = np.concatenate([np.cos(angles), -np.sin(angles)], axis=1) / math.sqrt(SEG)
    angles = (left * (right - SEG // 2) % (2 * SEG)) * (math.pi / SEG)
    weights = np.where(left == 0, 1.0, 2.0) / (math.sqrt(SEG) * SEGS)
    inverse = np.concatenate([weights * np.cos(angles), -weights * np.sin(angles)], axis=0)
    return forward.astype(ml_dtypes.bfloat16), inverse.astype(ml_dtypes.bfloat16)


def aligned(rows):
    return -(-rows // 16) * 16


def spectra(parts, fwd_ref, scaled, loose, spec, first):
    total = sum(part.shape[1] for part in parts)
    pitch = aligned(total)
    for s in range(SEGS):
        base = s * pitch
        for part in parts:
            count = part.shape[1]
            tiles = [part[QUADS * s + q].astype(jnp.float32) for q in range(QUADS)]
            squares = sum(tile * tile for tile in tiles)
            power = jnp.sum(squares, axis=1, keepdims=True) * (1.0 / SEG)
            gain = lax.rsqrt(power + 1e-05)
            for q, tile in enumerate(tiles):
                scaled[pl.ds(base, count), q * TILE:(q + 1) * TILE] = (tile * gain).astype(jnp.bfloat16)
            base += count
    for s in range(0, SEGS, 2):
        rows = scaled[pl.ds(s * pitch, 2 * pitch), :]
        both = jnp.dot(rows, fwd_ref[...], preferred_element_type=jnp.float32)
        for t in range(2):
            for c in range(2 * QUADS):
                half, g = divmod(c, QUADS)
                row = (half * (SEGS // 2) + s // 2) * 8 + t * QUADS + g
                loose[pl.ds(row, total, stride=PITCH), :] = both[
                    t * pitch:t * pitch + total, c * TILE:(c + 1) * TILE]

    def whiten(ch, carry):
        v = [loose[pl.ds(ch * PITCH + r * 8, 8), :] for r in range(SEGS)]
        level = sum(x * x for x in v)
        level = level + pltpu.roll(level, 4, 0)
        gain = lax.rsqrt(level * (1.0 / SEGS) + 0.5)
        for r in range(SEGS):
            spec[pl.ds(pl.multiple_of((first + ch) * ROWS + r * 8, 8), 8), :] = v[r] * gain
        return carry

    lax.fori_loop(0, total, whiten, 0, unroll=4)


def pair_products(count, idx_ref, spec, cross):
    low_half = lax.broadcasted_iota(jnp.int32, (8, TILE), 0) < QUADS

    def step(n, carry):
        for t in range(UNROLL):
            p = n * UNROLL + t
            i = pl.multiple_of(idx_ref[0, p], 8)
            j = pl.multiple_of(idx_ref[1, p], 8)
            real = imag = None
            for h in range(SEGS // 2):
                lr = spec[pl.ds(i + h * 8, 8), :]
                li = spec[pl.ds(i + (SEGS // 2 + h) * 8, 8), :]
                rr = spec[pl.ds(j + h * 8, 8), :]
                ri = spec[pl.ds(j + (SEGS // 2 + h) * 8, 8), :]
                if real is None:
                    real = lr * rr + li * ri
                    imag = li * rr - lr * ri
                else:
                    real = real + lr * rr + li * ri
                    imag = imag + li * rr - lr * ri
            real = real + pltpu.roll(real, QUADS, 0)
            imag = imag + pltpu.roll(imag, QUADS, 0)
            cross[pl.ds(pl.multiple_of(p * 8, 8), 8), :] = jnp.where(low_half, real, imag)
        return carry

    lax.fori_loop(0, (count + UNROLL - 1) // UNROLL, step, 0)


def own_kernel(own_ref, fwd_ref, kept, scaled, loose, spec, sem):
    spectra([own_ref], fwd_ref, scaled, loose, spec, 0)
    copy = pltpu.make_async_copy(spec, kept, sem)
    copy.start()
    copy.wait()


def pair_kernel(idx_ref, live_ref, h1_ref, h2_ref, kept, fwd_ref, inv_ref, out_ref,
                scaled, loose, spec, cross, stacks, sems):
    kept_copy = pltpu.make_async_copy(kept, spec.at[pl.ds(0, OWN * ROWS), :], sems.at[0])
    kept_copy.start()
    spectra([h1_ref, h2_ref], fwd_ref, scaled, loose, spec, OWN)
    kept_copy.wait()
    live = live_ref[0]
    pair_products(live, idx_ref, spec, cross)
    copies = []
    for b in range(CAP // BLOCK):
        rows = pl.ds(b * BLOCK, BLOCK)

        @pl.when(b * BLOCK < live)
        def _():
            columns = [cross[pl.ds(b * BLOCK * 8 + g, BLOCK, stride=8), :].astype(jnp.bfloat16) for g in range(8)]
            lagged = jnp.dot(
                jnp.concatenate(columns, axis=1), inv_ref[...], preferred_element_type=jnp.float32)
            slot = lax.broadcasted_iota(jnp.int32, (BLOCK, SEG), 0) + b * BLOCK
            stacks[rows, :] = jnp.where(slot < live, lagged, 0.0)

        @pl.when(b * BLOCK >= live)
        def _():
            stacks[rows, :] = jnp.zeros((BLOCK, SEG), jnp.float32)

        copies.append(pltpu.make_async_copy(stacks.at[rows, :], out_ref.at[rows, :], sems.at[1 + b]))
        copies[-1].start()
    for copy in copies:
        copy.wait()


def floats(*shape):
    return jax.ShapeDtypeStruct(shape, jnp.float32)


def own_spectra(own, fwd):
    return pl.pallas_call(
        own_kernel,
        out_shape=floats(OWN * ROWS, TILE),
        in_specs=[VMEM, VMEM],
        out_specs=HBM,
        scratch_shapes=[
            pltpu.VMEM((SEGS * OWN, SEG), jnp.bfloat16),
            pltpu.VMEM((OWN * PITCH + 8, TILE), jnp.float32),
            pltpu.VMEM((OWN * ROWS, TILE), jnp.float32),
            pltpu.SemaphoreType.DMA(()),
        ],
        compiler_params=pltpu.CompilerParams(vmem_limit_bytes=LIMIT),
        name="own_spectra",
    )(own, fwd)


def pair_stacks(idx, live, h1, h2, kept, fwd, inv):
    return pl.pallas_call(
        pair_kernel,
        out_shape=floats(CAP, SEG),
        in_specs=[SMEM, SMEM, VMEM, VMEM, HBM, VMEM, VMEM],
        out_specs=HBM,
        scratch_shapes=[
            pltpu.VMEM((SEGS * aligned(HALO), SEG), jnp.bfloat16),
            pltpu.VMEM((HALO * PITCH + 8, TILE), jnp.float32),
            pltpu.VMEM(((OWN + HALO) * ROWS, TILE), jnp.float32),
            pltpu.VMEM((CAP * 8, TILE), jnp.float32),
            pltpu.VMEM((CAP, SEG), jnp.float32),
            pltpu.SemaphoreType.DMA((1 + CAP // BLOCK,)),
        ],
        compiler_params=pltpu.CompilerParams(vmem_limit_bytes=LIMIT),
        name="pair_stacks",
    )(idx, live, h1, h2, kept, fwd, inv)


def turn_kernel(panels, part, whole, held, in_sems, out_sems):
    tiles, sections = panels.shape[:2]
    group = sections // TURNS
    loads, stores = [], []
    for a in range(tiles):
        for n in range(TURNS):
            rows = pl.ds(n * group, group)
            sem = in_sems.at[len(loads)]
            loads.append(pltpu.make_async_copy(panels.at[a, rows], held.at[a, rows], sem))
            loads[-1].start()
    for a in range(tiles):
        for n in range(TURNS):
            rows = pl.ds(n * group, group)
            loads[a * TURNS + n].wait()
            for turned in (whole, part):
                count = turned.shape[2]
                source = held.at[a, rows, pl.ds(0, count), :]
                stores.append(pltpu.make_async_copy(source, turned.at[rows, a], out_sems.at[len(stores)]))
                stores[-1].start()
    for store in stores:
        store.wait()


def turn(panels):
    tiles, sections, _, width = panels.shape
    return pl.pallas_call(
        turn_kernel,
        out_shape=[
            jax.ShapeDtypeStruct((sections, tiles, count, width), panels.dtype) for count in (REST, OWN)],
        in_specs=[HBM],
        out_specs=[HBM] * 2,
        scratch_shapes=[
            pltpu.VMEM(panels.shape, panels.dtype),
            pltpu.SemaphoreType.DMA((tiles * TURNS,)),
            pltpu.SemaphoreType.DMA((2 * tiles * TURNS,)),
        ],
        compiler_params=pltpu.CompilerParams(vmem_limit_bytes=62 << 20),
        name="turn",
    )(panels)


def from_ahead(block, axis, distance):
    devices = range(lax.axis_size(axis))
    route = [(i + distance, i) for i in devices if i + distance in devices]
    return lax.ppermute(block, axis, route)


def by_section(block):
    rows = lax.all_to_all(block, "tm", split_axis=0, concat_axis=0, tiled=True)
    return rows.reshape(-1, *block.shape[2:])


def per_device(panels, pair_list, pair_count):
    fwd, inv = (jnp.asarray(table) for table in tables())
    offset = (lax.axis_index("tm") * lax.axis_size("pairs") + lax.axis_index("pairs")) * OWN
    idx = (pair_list - offset) * ROWS
    part, whole = turn(panels)
    h2_turned = from_ahead(part, "pairs", 2)
    own = by_section(whole)
    h1 = from_ahead(own, "pairs", 1)
    h2 = by_section(h2_turned)
    kept = own_spectra(own, fwd)
    return pair_stacks(idx, pair_count, h1, h2, kept, fwd, inv)


def solution(mesh):
    return jax.shard_map(
        per_device,
        mesh=mesh,
        in_specs=(P("tm", None, "pairs", None), P(None, ("tm", "pairs")), P(("tm", "pairs"))),
        out_specs=P(("tm", "pairs"), None),
        check_vma=False,
    )
```

```python
import math

import jax
import jax.numpy as jnp
import ml_dtypes
import numpy as np
from jax import lax
from jax.experimental import pallas as pl
from jax.experimental.pallas import tpu as pltpu
from jax.sharding import PartitionSpec as P

NB = 100
SEG = 512
SEGS = 12
TILE = 128
QUADS = SEG // TILE
OWN = 64
HALO = 104
REST = HALO - OWN
ROWS = SEGS * 8
PITCH = ROWS + 1
CAP = 1024
UNROLL = 32
LIMIT = 50 << 20
LAST_LIMIT = 52633 << 10
TURNS = 2
BLOCK = 256
VMEM = pl.BlockSpec(memory_space=pltpu.VMEM)
SMEM = pl.BlockSpec(memory_space=pltpu.SMEM)
HBM = pl.BlockSpec(memory_space=pltpu.HBM)


def tables():
    left = np.arange(SEG)[:, None]
    right = np.arange(SEG)[None, :]
    angles = (left * right % (2 * SEG)) * (math.pi / SEG)
    forward = np.concatenate([np.cos(angles), -np.sin(angles)], axis=1) / math.sqrt(SEG)
    angles = (left * (right - SEG // 2) % (2 * SEG)) * (math.pi / SEG)
    weights = np.where(left == 0, 1.0, 2.0) / (math.sqrt(SEG) * SEGS)
    inverse = np.concatenate([weights * np.cos(angles), -weights * np.sin(angles)], axis=0)
    return forward.astype(ml_dtypes.bfloat16), inverse.astype(ml_dtypes.bfloat16)


def aligned(rows):
    return -(-rows // 16) * 16


def spectra(parts, fwd_ref, scaled, loose, spec, first):
    total = sum(part.shape[1] for part in parts)
    pitch = aligned(total)
    for s in range(SEGS):
        base = s * pitch
        for part in parts:
            count = part.shape[1]
            tiles = [part[QUADS * s + q].astype(jnp.float32) for q in range(QUADS)]
            squares = sum(tile * tile for tile in tiles)
            power = jnp.sum(squares, axis=1, keepdims=True) * (1.0 / SEG)
            gain = lax.rsqrt(power + 1e-05)
            for q, tile in enumerate(tiles):
                scaled[pl.ds(base, count), q * TILE:(q + 1) * TILE] = (tile * gain).astype(jnp.bfloat16)
            base += count
    for s in range(0, SEGS, 2):
        rows = scaled[pl.ds(s * pitch, 2 * pitch), :]
        both = jnp.dot(rows, fwd_ref[...], preferred_element_type=jnp.float32)
        for t in range(2):
            for c in range(2 * QUADS):
                half, g = divmod(c, QUADS)
                row = (half * (SEGS // 2) + s // 2) * 8 + t * QUADS + g
                loose[pl.ds(row, total, stride=PITCH), :] = both[
                    t * pitch:t * pitch + total, c * TILE:(c + 1) * TILE]

    def whiten(ch, carry):
        v = [loose[pl.ds(ch * PITCH + r * 8, 8), :] for r in range(SEGS)]
        level = sum(x * x for x in v)
        level = level + pltpu.roll(level, 4, 0)
        gain = lax.rsqrt(level * (1.0 / SEGS) + 0.5)
        for r in range(SEGS):
            spec[pl.ds(pl.multiple_of((first + ch) * ROWS + r * 8, 8), 8), :] = v[r] * gain
        return carry

    lax.fori_loop(0, total, whiten, 0, unroll=4)


def pair_products(count, idx_ref, spec, cross):
    low_half = lax.broadcasted_iota(jnp.int32, (8, TILE), 0) < QUADS

    def step(n, carry):
        for t in range(UNROLL):
            p = n * UNROLL + t
            i = pl.multiple_of(idx_ref[0, p], 8)
            j = pl.multiple_of(idx_ref[1, p], 8)
            real = imag = None
            for h in range(SEGS // 2):
                lr = spec[pl.ds(i + h * 8, 8), :]
                li = spec[pl.ds(i + (SEGS // 2 + h) * 8, 8), :]
                rr = spec[pl.ds(j + h * 8, 8), :]
                ri = spec[pl.ds(j + (SEGS // 2 + h) * 8, 8), :]
                if real is None:
                    real = lr * rr + li * ri
                    imag = li * rr - lr * ri
                else:
                    real = real + lr * rr + li * ri
                    imag = imag + li * rr - lr * ri
            real = real + pltpu.roll(real, QUADS, 0)
            imag = imag + pltpu.roll(imag, QUADS, 0)
            cross[pl.ds(pl.multiple_of(p * 8, 8), 8), :] = jnp.where(low_half, real, imag)
        return carry

    lax.fori_loop(0, (count + UNROLL - 1) // UNROLL, step, 0)


def own_kernel(own_ref, fwd_ref, kept, scaled, loose, spec, sem):
    spectra([own_ref], fwd_ref, scaled, loose, spec, 0)
    copy = pltpu.make_async_copy(spec, kept, sem)
    copy.start()
    copy.wait()


def pair_kernel(idx_ref, live_ref, h1_ref, h2_ref, kept, fwd_ref, inv_table, out_ref,
                scaled, loose, spec, cross, stacks, inv_ref, sems):
    kept_copy = pltpu.make_async_copy(kept, spec.at[pl.ds(0, OWN * ROWS), :], sems.at[0])
    kept_copy.start()
    inv_copy = pltpu.make_async_copy(inv_table, inv_ref, sems.at[1 + CAP // BLOCK])
    inv_copy.start()
    spectra([h1_ref, h2_ref], fwd_ref, scaled, loose, spec, OWN)
    kept_copy.wait()
    live = live_ref[0]
    pair_products(live, idx_ref, spec, cross)
    inv_copy.wait()
    copies = []
    for b in range(CAP // BLOCK):
        rows = pl.ds(b * BLOCK, BLOCK)

        @pl.when(b * BLOCK < live)
        def _():
            columns = [cross[pl.ds(b * BLOCK * 8 + g, BLOCK, stride=8), :].astype(jnp.bfloat16) for g in range(8)]
            lagged = jnp.dot(
                jnp.concatenate(columns, axis=1), inv_ref[...], preferred_element_type=jnp.float32)
            slot = lax.broadcasted_iota(jnp.int32, (BLOCK, SEG), 0) + b * BLOCK
            stacks[rows, :] = jnp.where(slot < live, lagged, 0.0)

        @pl.when(b * BLOCK >= live)
        def _():
            stacks[rows, :] = jnp.zeros((BLOCK, SEG), jnp.float32)

        copies.append(pltpu.make_async_copy(stacks.at[rows, :], out_ref.at[rows, :], sems.at[1 + b]))
        copies[-1].start()
    for copy in copies:
        copy.wait()


def floats(*shape):
    return jax.ShapeDtypeStruct(shape, jnp.float32)


def own_spectra(own, fwd):
    return pl.pallas_call(
        own_kernel,
        out_shape=floats(OWN * ROWS, TILE),
        in_specs=[VMEM, VMEM],
        out_specs=HBM,
        scratch_shapes=[
            pltpu.VMEM((SEGS * OWN, SEG), jnp.bfloat16),
            pltpu.VMEM((OWN * PITCH + 8, TILE), jnp.float32),
            pltpu.VMEM((OWN * ROWS, TILE), jnp.float32),
            pltpu.SemaphoreType.DMA(()),
        ],
        compiler_params=pltpu.CompilerParams(vmem_limit_bytes=LIMIT),
        name="own_spectra",
    )(own, fwd)


def pair_stacks(idx, live, h1, h2, kept, fwd, inv):
    return pl.pallas_call(
        pair_kernel,
        out_shape=floats(CAP, SEG),
        in_specs=[SMEM, SMEM, VMEM, VMEM, HBM, VMEM, HBM],
        out_specs=HBM,
        scratch_shapes=[
            pltpu.VMEM((SEGS * aligned(HALO), SEG), jnp.bfloat16),
            pltpu.VMEM((HALO * PITCH + 8, TILE), jnp.float32),
            pltpu.VMEM(((OWN + HALO) * ROWS, TILE), jnp.float32),
            pltpu.VMEM((CAP * 8, TILE), jnp.float32),
            pltpu.VMEM((CAP, SEG), jnp.float32),
            pltpu.VMEM((2 * SEG, SEG), jnp.bfloat16),
            pltpu.SemaphoreType.DMA((2 + CAP // BLOCK,)),
        ],
        compiler_params=pltpu.CompilerParams(vmem_limit_bytes=LAST_LIMIT),
        name="pair_stacks",
    )(idx, live, h1, h2, kept, fwd, inv)


def turn_kernel(panels, part, whole, held, in_sems, out_sems):
    tiles, sections = panels.shape[:2]
    group = sections // TURNS
    loads, stores = [], []
    for a in range(tiles):
        for n in range(TURNS):
            rows = pl.ds(n * group, group)
            sem = in_sems.at[len(loads)]
            loads.append(pltpu.make_async_copy(panels.at[a, rows], held.at[a, rows], sem))
            loads[-1].start()
    for a in range(tiles):
        for n in range(TURNS):
            rows = pl.ds(n * group, group)
            loads[a * TURNS + n].wait()
            for turned in (whole, part):
                count = turned.shape[2]
                source = held.at[a, rows, pl.ds(0, count), :]
                stores.append(pltpu.make_async_copy(source, turned.at[rows, a], out_sems.at[len(stores)]))
                stores[-1].start()
    for store in stores:
        store.wait()


def turn(panels):
    tiles, sections, _, width = panels.shape
    return pl.pallas_call(
        turn_kernel,
        out_shape=[
            jax.ShapeDtypeStruct((sections, tiles, count, width), panels.dtype) for count in (REST, OWN)],
        in_specs=[HBM],
        out_specs=[HBM] * 2,
        scratch_shapes=[
            pltpu.VMEM(panels.shape, panels.dtype),
            pltpu.SemaphoreType.DMA((tiles * TURNS,)),
            pltpu.SemaphoreType.DMA((2 * tiles * TURNS,)),
        ],
        compiler_params=pltpu.CompilerParams(vmem_limit_bytes=62 << 20),
        name="turn",
    )(panels)


def from_ahead(block, axis, distance):
    devices = range(lax.axis_size(axis))
    route = [(i + distance, i) for i in devices if i + distance in devices]
    return lax.ppermute(block, axis, route)


def by_section(block):
    rows = lax.all_to_all(block, "tm", split_axis=0, concat_axis=0, tiled=True)
    return rows.reshape(-1, *block.shape[2:])


def per_device(panels, pair_list, pair_count):
    fwd, inv = (jnp.asarray(table) for table in tables())
    offset = (lax.axis_index("tm") * lax.axis_size("pairs") + lax.axis_index("pairs")) * OWN
    idx = (pair_list - offset) * ROWS
    part, whole = turn(panels)
    h2_turned = from_ahead(part, "pairs", 2)
    own = by_section(whole)
    h1 = from_ahead(own, "pairs", 1)
    h2 = by_section(h2_turned)
    kept = own_spectra(own, fwd)
    return pair_stacks(idx, pair_count, h1, h2, kept, fwd, inv)


def solution(mesh):
    return jax.shard_map(
        per_device,
        mesh=mesh,
        in_specs=(P("tm", None, "pairs", None), P(None, ("tm", "pairs")), P(("tm", "pairs"))),
        out_specs=P(("tm", "pairs"), None),
        check_vma=False,
    )
```

```python
import math

import jax
import jax.numpy as jnp
import ml_dtypes
import numpy as np
from jax import lax
from jax.experimental import pallas as pl
from jax.experimental.pallas import tpu as pltpu
from jax.sharding import PartitionSpec as P

NB = 100
SEG = 512
SEGS = 12
TILE = 128
QUADS = SEG // TILE
OWN = 64
HALO = 104
REST = HALO - OWN
ROWS = SEGS * 8
PITCH = ROWS + 1
CAP = 1024
UNROLL = 64
LIMIT = 50 << 20
LAST_LIMIT = 52633 << 10
TURNS = 2
BLOCK = 256
VMEM = pl.BlockSpec(memory_space=pltpu.VMEM)
SMEM = pl.BlockSpec(memory_space=pltpu.SMEM)
HBM = pl.BlockSpec(memory_space=pltpu.HBM)


def tables():
    left = np.arange(SEG)[:, None]
    right = np.arange(SEG)[None, :]
    angles = (left * right % (2 * SEG)) * (math.pi / SEG)
    forward = np.concatenate([np.cos(angles), -np.sin(angles)], axis=1) / math.sqrt(SEG)
    angles = (left * (right - SEG // 2) % (2 * SEG)) * (math.pi / SEG)
    weights = np.where(left == 0, 1.0, 2.0) / (math.sqrt(SEG) * SEGS)
    inverse = np.concatenate([weights * np.cos(angles), -weights * np.sin(angles)], axis=0)
    return forward.astype(ml_dtypes.bfloat16), inverse.astype(ml_dtypes.bfloat16)


def aligned(rows):
    return -(-rows // 16) * 16


def spectra(parts, fwd_ref, scaled, loose, spec, first):
    total = sum(part.shape[1] for part in parts)
    pitch = aligned(total)
    for s in range(SEGS):
        base = s * pitch
        for part in parts:
            count = part.shape[1]
            tiles = [part[QUADS * s + q].astype(jnp.float32) for q in range(QUADS)]
            squares = sum(tile * tile for tile in tiles)
            power = jnp.sum(squares, axis=1, keepdims=True) * (1.0 / SEG)
            gain = lax.rsqrt(power + 1e-05)
            for q, tile in enumerate(tiles):
                scaled[pl.ds(base, count), q * TILE:(q + 1) * TILE] = (tile * gain).astype(jnp.bfloat16)
            base += count
    for s in range(0, SEGS, 2):
        rows = scaled[pl.ds(s * pitch, 2 * pitch), :]
        both = jnp.dot(rows, fwd_ref[...], preferred_element_type=jnp.float32)
        for t in range(2):
            for c in range(2 * QUADS):
                half, g = divmod(c, QUADS)
                row = (half * (SEGS // 2) + s // 2) * 8 + t * QUADS + g
                loose[pl.ds(row, total, stride=PITCH), :] = both[
                    t * pitch:t * pitch + total, c * TILE:(c + 1) * TILE]

    def whiten(ch, carry):
        v = [loose[pl.ds(ch * PITCH + r * 8, 8), :] for r in range(SEGS)]
        level = sum(x * x for x in v)
        level = level + pltpu.roll(level, 4, 0)
        gain = lax.rsqrt(level * (1.0 / SEGS) + 0.5)
        for r in range(SEGS):
            spec[pl.ds(pl.multiple_of((first + ch) * ROWS + r * 8, 8), 8), :] = v[r] * gain
        return carry

    lax.fori_loop(0, total, whiten, 0, unroll=4)


def pair_products(count, idx_ref, spec, cross):
    low_half = lax.broadcasted_iota(jnp.int32, (8, TILE), 0) < QUADS

    def step(n, carry):
        for t in range(UNROLL):
            p = n * UNROLL + t
            i = pl.multiple_of(idx_ref[0, p], 8)
            j = pl.multiple_of(idx_ref[1, p], 8)
            real = imag = None
            for h in range(SEGS // 2):
                lr = spec[pl.ds(i + h * 8, 8), :]
                li = spec[pl.ds(i + (SEGS // 2 + h) * 8, 8), :]
                rr = spec[pl.ds(j + h * 8, 8), :]
                ri = spec[pl.ds(j + (SEGS // 2 + h) * 8, 8), :]
                if real is None:
                    real = lr * rr + li * ri
                    imag = li * rr - lr * ri
                else:
                    real = real + lr * rr + li * ri
                    imag = imag + li * rr - lr * ri
            real = real + pltpu.roll(real, QUADS, 0)
            imag = imag + pltpu.roll(imag, QUADS, 0)
            cross[pl.ds(pl.multiple_of(p * 8, 8), 8), :] = jnp.where(low_half, real, imag)
        return carry

    lax.fori_loop(0, (count + UNROLL - 1) // UNROLL, step, 0)


def own_kernel(own_ref, fwd_ref, kept, scaled, loose, spec, sem):
    spectra([own_ref], fwd_ref, scaled, loose, spec, 0)
    copy = pltpu.make_async_copy(spec, kept, sem)
    copy.start()
    copy.wait()


def pair_kernel(idx_ref, live_ref, h1_ref, h2_ref, kept, fwd_ref, inv_table, out_ref,
                scaled, loose, spec, cross, stacks, inv_ref, sems):
    kept_copy = pltpu.make_async_copy(kept, spec.at[pl.ds(0, OWN * ROWS), :], sems.at[0])
    kept_copy.start()
    inv_copy = pltpu.make_async_copy(inv_table, inv_ref, sems.at[1 + CAP // BLOCK])
    inv_copy.start()
    spectra([h1_ref, h2_ref], fwd_ref, scaled, loose, spec, OWN)
    kept_copy.wait()
    live = live_ref[0]
    pair_products(live, idx_ref, spec, cross)
    inv_copy.wait()
    copies = []
    for b in range(CAP // BLOCK):
        rows = pl.ds(b * BLOCK, BLOCK)

        @pl.when(b * BLOCK < live)
        def _():
            columns = [cross[pl.ds(b * BLOCK * 8 + g, BLOCK, stride=8), :].astype(jnp.bfloat16) for g in range(8)]
            lagged = jnp.dot(
                jnp.concatenate(columns, axis=1), inv_ref[...], preferred_element_type=jnp.float32)
            slot = lax.broadcasted_iota(jnp.int32, (BLOCK, SEG), 0) + b * BLOCK
            stacks[rows, :] = jnp.where(slot < live, lagged, 0.0)

        @pl.when(b * BLOCK >= live)
        def _():
            stacks[rows, :] = jnp.zeros((BLOCK, SEG), jnp.float32)

        copies.append(pltpu.make_async_copy(stacks.at[rows, :], out_ref.at[rows, :], sems.at[1 + b]))
        copies[-1].start()
    for copy in copies:
        copy.wait()


def floats(*shape):
    return jax.ShapeDtypeStruct(shape, jnp.float32)


def own_spectra(own, fwd):
    return pl.pallas_call(
        own_kernel,
        out_shape=floats(OWN * ROWS, TILE),
        in_specs=[VMEM, VMEM],
        out_specs=HBM,
        scratch_shapes=[
            pltpu.VMEM((SEGS * OWN, SEG), jnp.bfloat16),
            pltpu.VMEM((OWN * PITCH + 8, TILE), jnp.float32),
            pltpu.VMEM((OWN * ROWS, TILE), jnp.float32),
            pltpu.SemaphoreType.DMA(()),
        ],
        compiler_params=pltpu.CompilerParams(vmem_limit_bytes=LIMIT),
        name="own_spectra",
    )(own, fwd)


def pair_stacks(idx, live, h1, h2, kept, fwd, inv):
    return pl.pallas_call(
        pair_kernel,
        out_shape=floats(CAP, SEG),
        in_specs=[SMEM, SMEM, VMEM, VMEM, HBM, VMEM, HBM],
        out_specs=HBM,
        scratch_shapes=[
            pltpu.VMEM((SEGS * aligned(HALO), SEG), jnp.bfloat16),
            pltpu.VMEM((HALO * PITCH + 8, TILE), jnp.float32),
            pltpu.VMEM(((OWN + HALO) * ROWS, TILE), jnp.float32),
            pltpu.VMEM((CAP * 8, TILE), jnp.float32),
            pltpu.VMEM((CAP, SEG), jnp.float32),
            pltpu.VMEM((2 * SEG, SEG), jnp.bfloat16),
            pltpu.SemaphoreType.DMA((2 + CAP // BLOCK,)),
        ],
        compiler_params=pltpu.CompilerParams(vmem_limit_bytes=LAST_LIMIT),
        name="pair_stacks",
    )(idx, live, h1, h2, kept, fwd, inv)


def turn_kernel(panels, part, whole, held, in_sems, out_sems):
    tiles, sections = panels.shape[:2]
    group = sections // TURNS
    loads, stores = [], []
    for a in range(tiles):
        for n in range(TURNS):
            rows = pl.ds(n * group, group)
            sem = in_sems.at[len(loads)]
            loads.append(pltpu.make_async_copy(panels.at[a, rows], held.at[a, rows], sem))
            loads[-1].start()
    for a in range(tiles):
        for n in range(TURNS):
            rows = pl.ds(n * group, group)
            loads[a * TURNS + n].wait()
            for turned in (whole, part):
                count = turned.shape[2]
                source = held.at[a, rows, pl.ds(0, count), :]
                stores.append(pltpu.make_async_copy(source, turned.at[rows, a], out_sems.at[len(stores)]))
                stores[-1].start()
    for store in stores:
        store.wait()


def turn(panels):
    tiles, sections, _, width = panels.shape
    return pl.pallas_call(
        turn_kernel,
        out_shape=[
            jax.ShapeDtypeStruct((sections, tiles, count, width), panels.dtype) for count in (REST, OWN)],
        in_specs=[HBM],
        out_specs=[HBM] * 2,
        scratch_shapes=[
            pltpu.VMEM(panels.shape, panels.dtype),
            pltpu.SemaphoreType.DMA((tiles * TURNS,)),
            pltpu.SemaphoreType.DMA((2 * tiles * TURNS,)),
        ],
        compiler_params=pltpu.CompilerParams(vmem_limit_bytes=62 << 20),
        name="turn",
    )(panels)


def from_ahead(block, axis, distance):
    devices = range(lax.axis_size(axis))
    route = [(i + distance, i) for i in devices if i + distance in devices]
    return lax.ppermute(block, axis, route)


def by_section(block):
    rows = lax.all_to_all(block, "tm", split_axis=0, concat_axis=0, tiled=True)
    return rows.reshape(-1, *block.shape[2:])


def per_device(panels, pair_list, pair_count):
    fwd, inv = (jnp.asarray(table) for table in tables())
    offset = (lax.axis_index("tm") * lax.axis_size("pairs") + lax.axis_index("pairs")) * OWN
    idx = (pair_list - offset) * ROWS
    part, whole = turn(panels)
    h2_turned = from_ahead(part, "pairs", 2)
    own = by_section(whole)
    h1 = from_ahead(own, "pairs", 1)
    h2 = by_section(h2_turned)
    kept = own_spectra(own, fwd)
    return pair_stacks(idx, pair_count, h1, h2, kept, fwd, inv)


def solution(mesh):
    return jax.shard_map(
        per_device,
        mesh=mesh,
        in_specs=(P("tm", None, "pairs", None), P(None, ("tm", "pairs")), P(("tm", "pairs"))),
        out_specs=P(("tm", "pairs"), None),
        check_vma=False,
    )
```

```python
import math

import jax
import jax.numpy as jnp
import ml_dtypes
import numpy as np
from jax import lax
from jax.experimental import pallas as pl
from jax.experimental.pallas import tpu as pltpu
from jax.sharding import PartitionSpec as P

NB = 100
SEG = 512
SEGS = 12
TILE = 128
QUADS = SEG // TILE
OWN = 64
HALO = 104
REST = HALO - OWN
ROWS = SEGS * 8
PITCH = ROWS + 1
CAP = 1024
UNROLL = 128
LIMIT = 50 << 20
LAST_LIMIT = 52633 << 10
TURNS = 2
BLOCK = 256
VMEM = pl.BlockSpec(memory_space=pltpu.VMEM)
SMEM = pl.BlockSpec(memory_space=pltpu.SMEM)
HBM = pl.BlockSpec(memory_space=pltpu.HBM)


def tables():
    left = np.arange(SEG)[:, None]
    right = np.arange(SEG)[None, :]
    angles = (left * right % (2 * SEG)) * (math.pi / SEG)
    forward = np.concatenate([np.cos(angles), -np.sin(angles)], axis=1) / math.sqrt(SEG)
    angles = (left * (right - SEG // 2) % (2 * SEG)) * (math.pi / SEG)
    weights = np.where(left == 0, 1.0, 2.0) / (math.sqrt(SEG) * SEGS)
    inverse = np.concatenate([weights * np.cos(angles), -weights * np.sin(angles)], axis=0)
    return forward.astype(ml_dtypes.bfloat16), inverse.astype(ml_dtypes.bfloat16)


def aligned(rows):
    return -(-rows // 16) * 16


def spectra(parts, fwd_ref, scaled, loose, spec, first):
    total = sum(part.shape[1] for part in parts)
    pitch = aligned(total)
    for s in range(SEGS):
        base = s * pitch
        for part in parts:
            count = part.shape[1]
            tiles = [part[QUADS * s + q].astype(jnp.float32) for q in range(QUADS)]
            squares = sum(tile * tile for tile in tiles)
            power = jnp.sum(squares, axis=1, keepdims=True) * (1.0 / SEG)
            gain = lax.rsqrt(power + 1e-05)
            for q, tile in enumerate(tiles):
                scaled[pl.ds(base, count), q * TILE:(q + 1) * TILE] = (tile * gain).astype(jnp.bfloat16)
            base += count
    for s in range(0, SEGS, 2):
        rows = scaled[pl.ds(s * pitch, 2 * pitch), :]
        both = jnp.dot(rows, fwd_ref[...], preferred_element_type=jnp.float32)
        for t in range(2):
            for c in range(2 * QUADS):
                half, g = divmod(c, QUADS)
                row = (half * (SEGS // 2) + s // 2) * 8 + t * QUADS + g
                loose[pl.ds(row, total, stride=PITCH), :] = both[
                    t * pitch:t * pitch + total, c * TILE:(c + 1) * TILE]

    def whiten(ch, carry):
        v = [loose[pl.ds(ch * PITCH + r * 8, 8), :] for r in range(SEGS)]
        level = sum(x * x for x in v)
        level = level + pltpu.roll(level, 4, 0)
        gain = lax.rsqrt(level * (1.0 / SEGS) + 0.5)
        for r in range(SEGS):
            spec[pl.ds(pl.multiple_of((first + ch) * ROWS + r * 8, 8), 8), :] = v[r] * gain
        return carry

    lax.fori_loop(0, total, whiten, 0, unroll=4)


def pair_products(count, idx_ref, spec, cross):
    low_half = lax.broadcasted_iota(jnp.int32, (8, TILE), 0) < QUADS

    def step(n, carry):
        for t in range(UNROLL):
            p = n * UNROLL + t
            i = pl.multiple_of(idx_ref[0, p], 8)
            j = pl.multiple_of(idx_ref[1, p], 8)
            real = imag = None
            for h in range(SEGS // 2):
                lr = spec[pl.ds(i + h * 8, 8), :]
                li = spec[pl.ds(i + (SEGS // 2 + h) * 8, 8), :]
                rr = spec[pl.ds(j + h * 8, 8), :]
                ri = spec[pl.ds(j + (SEGS // 2 + h) * 8, 8), :]
                if real is None:
                    real = lr * rr + li * ri
                    imag = li * rr - lr * ri
                else:
                    real = real + lr * rr + li * ri
                    imag = imag + li * rr - lr * ri
            real = real + pltpu.roll(real, QUADS, 0)
            imag = imag + pltpu.roll(imag, QUADS, 0)
            cross[pl.ds(pl.multiple_of(p * 8, 8), 8), :] = jnp.where(low_half, real, imag)
        return carry

    lax.fori_loop(0, (count + UNROLL - 1) // UNROLL, step, 0)


def own_kernel(own_ref, fwd_ref, kept, scaled, loose, spec, sem):
    spectra([own_ref], fwd_ref, scaled, loose, spec, 0)
    copy = pltpu.make_async_copy(spec, kept, sem)
    copy.start()
    copy.wait()


def pair_kernel(idx_ref, live_ref, h1_ref, h2_ref, kept, fwd_ref, inv_table, out_ref,
                scaled, loose, spec, cross, stacks, inv_ref, sems):
    kept_copy = pltpu.make_async_copy(kept, spec.at[pl.ds(0, OWN * ROWS), :], sems.at[0])
    kept_copy.start()
    inv_copy = pltpu.make_async_copy(inv_table, inv_ref, sems.at[1 + CAP // BLOCK])
    inv_copy.start()
    spectra([h1_ref, h2_ref], fwd_ref, scaled, loose, spec, OWN)
    kept_copy.wait()
    live = live_ref[0]
    pair_products(live, idx_ref, spec, cross)
    inv_copy.wait()
    copies = []
    for b in range(CAP // BLOCK):
        rows = pl.ds(b * BLOCK, BLOCK)

        @pl.when(b * BLOCK < live)
        def _():
            columns = [cross[pl.ds(b * BLOCK * 8 + g, BLOCK, stride=8), :].astype(jnp.bfloat16) for g in range(8)]
            lagged = jnp.dot(
                jnp.concatenate(columns, axis=1), inv_ref[...], preferred_element_type=jnp.float32)
            slot = lax.broadcasted_iota(jnp.int32, (BLOCK, SEG), 0) + b * BLOCK
            stacks[rows, :] = jnp.where(slot < live, lagged, 0.0)

        @pl.when(b * BLOCK >= live)
        def _():
            stacks[rows, :] = jnp.zeros((BLOCK, SEG), jnp.float32)

        copies.append(pltpu.make_async_copy(stacks.at[rows, :], out_ref.at[rows, :], sems.at[1 + b]))
        copies[-1].start()
    for copy in copies:
        copy.wait()


def floats(*shape):
    return jax.ShapeDtypeStruct(shape, jnp.float32)


def own_spectra(own, fwd):
    return pl.pallas_call(
        own_kernel,
        out_shape=floats(OWN * ROWS, TILE),
        in_specs=[VMEM, VMEM],
        out_specs=HBM,
        scratch_shapes=[
            pltpu.VMEM((SEGS * OWN, SEG), jnp.bfloat16),
            pltpu.VMEM((OWN * PITCH + 8, TILE), jnp.float32),
            pltpu.VMEM((OWN * ROWS, TILE), jnp.float32),
            pltpu.SemaphoreType.DMA(()),
        ],
        compiler_params=pltpu.CompilerParams(vmem_limit_bytes=LIMIT),
        name="own_spectra",
    )(own, fwd)


def pair_stacks(idx, live, h1, h2, kept, fwd, inv):
    return pl.pallas_call(
        pair_kernel,
        out_shape=floats(CAP, SEG),
        in_specs=[SMEM, SMEM, VMEM, VMEM, HBM, VMEM, HBM],
        out_specs=HBM,
        scratch_shapes=[
            pltpu.VMEM((SEGS * aligned(HALO), SEG), jnp.bfloat16),
            pltpu.VMEM((HALO * PITCH + 8, TILE), jnp.float32),
            pltpu.VMEM(((OWN + HALO) * ROWS, TILE), jnp.float32),
            pltpu.VMEM((CAP * 8, TILE), jnp.float32),
            pltpu.VMEM((CAP, SEG), jnp.float32),
            pltpu.VMEM((2 * SEG, SEG), jnp.bfloat16),
            pltpu.SemaphoreType.DMA((2 + CAP // BLOCK,)),
        ],
        compiler_params=pltpu.CompilerParams(vmem_limit_bytes=LAST_LIMIT),
        name="pair_stacks",
    )(idx, live, h1, h2, kept, fwd, inv)


def turn_kernel(panels, part, whole, held, in_sems, out_sems):
    tiles, sections = panels.shape[:2]
    group = sections // TURNS
    loads, stores = [], []
    for a in range(tiles):
        for n in range(TURNS):
            rows = pl.ds(n * group, group)
            sem = in_sems.at[len(loads)]
            loads.append(pltpu.make_async_copy(panels.at[a, rows], held.at[a, rows], sem))
            loads[-1].start()
    for a in range(tiles):
        for n in range(TURNS):
            rows = pl.ds(n * group, group)
            loads[a * TURNS + n].wait()
            for turned in (whole, part):
                count = turned.shape[2]
                source = held.at[a, rows, pl.ds(0, count), :]
                stores.append(pltpu.make_async_copy(source, turned.at[rows, a], out_sems.at[len(stores)]))
                stores[-1].start()
    for store in stores:
        store.wait()


def turn(panels):
    tiles, sections, _, width = panels.shape
    return pl.pallas_call(
        turn_kernel,
        out_shape=[
            jax.ShapeDtypeStruct((sections, tiles, count, width), panels.dtype) for count in (REST, OWN)],
        in_specs=[HBM],
        out_specs=[HBM] * 2,
        scratch_shapes=[
            pltpu.VMEM(panels.shape, panels.dtype),
            pltpu.SemaphoreType.DMA((tiles * TURNS,)),
            pltpu.SemaphoreType.DMA((2 * tiles * TURNS,)),
        ],
        compiler_params=pltpu.CompilerParams(vmem_limit_bytes=62 << 20),
        name="turn",
    )(panels)


def from_ahead(block, axis, distance):
    devices = range(lax.axis_size(axis))
    route = [(i + distance, i) for i in devices if i + distance in devices]
    return lax.ppermute(block, axis, route)


def by_section(block):
    rows = lax.all_to_all(block, "tm", split_axis=0, concat_axis=0, tiled=True)
    return rows.reshape(-1, *block.shape[2:])


def per_device(panels, pair_list, pair_count):
    fwd, inv = (jnp.asarray(table) for table in tables())
    offset = (lax.axis_index("tm") * lax.axis_size("pairs") + lax.axis_index("pairs")) * OWN
    idx = (pair_list - offset) * ROWS
    part, whole = turn(panels)
    h2_turned = from_ahead(part, "pairs", 2)
    own = by_section(whole)
    h1 = from_ahead(own, "pairs", 1)
    h2 = by_section(h2_turned)
    kept = own_spectra(own, fwd)
    return pair_stacks(idx, pair_count, h1, h2, kept, fwd, inv)


def solution(mesh):
    return jax.shard_map(
        per_device,
        mesh=mesh,
        in_specs=(P("tm", None, "pairs", None), P(None, ("tm", "pairs")), P(("tm", "pairs"))),
        out_specs=P(("tm", "pairs"), None),
        check_vma=False,
    )
```
